32 devices in a mesh: sec: 2 (over x), lat: 16 (over z, y, core).
Axes of the slice: x: 2, y: 2, z: 4, core: 2. Of those that a mesh axis runs over, the one named last changes fastest.
Arguments:
- resid_in: bfloat16 [4, 128, 2048], P('sec', None, 'lat'), may hold values from -6 to 6
- mlp_out: bfloat16 [4, 128, 2048], P('sec', None, 'lat'), may hold values from -6 to 6
- enc_weight: bfloat16 [4, 2048, 1024], P('sec', None, 'lat'), may hold values from -0.125 to 0.125
- enc_bias: float32 [4, 1024], P('sec', 'lat'), may hold values from -3 to 3
- thresholds: int32 [4, 1024], P('sec', 'lat'), may hold values from 0 to 3
- same_dec: bfloat16 [4, 1024, 2048], P('sec', 'lat'), may hold values from -0.1875 to 0.1875
- next_dec: bfloat16 [2, 1024, 2048], P('sec', 'lat'), may hold values from -0.1875 to 0.1875
- cross_dec: bfloat16 [2, 2, 1024, 2048], P('sec', None, 'lat'), may hold values from -0.1875 to 0.1875
Outputs:
- mean_square: float32 [], replicated
- grad_enc: bfloat16 [4, 2048, 1024], P('sec', None, 'lat')
- grad_bias: float32 [4, 1024], P('sec', 'lat')
- grad_same: bfloat16 [4, 1024, 2048], P('sec', 'lat')
- grad_next: bfloat16 [2, 1024, 2048], P('sec', 'lat')
- grad_cross: bfloat16 [2, 2, 1024, 2048], P('sec', None, 'lat')
The draws below stay inside these ranges and needn't reach their ends.
All inputs are finite; a program needn't handle non-finite values.
Results may differ from the reference program's by a relative error of at most 0.0059.
Values may be sent and summed in bfloat16 or wider, within the bound.
No kernel may reach another device: no remote copies, remote signals or barrier semaphores. Data moves between devices by JAX's collectives and lax.ppermute only.
A program may use at most 64 MiB of HBM per device.

```python
import jax
import jax.numpy as jnp

D = 2048
LAYERS = 4
TOKENS = 128
LATENTS = 1024


def with_ends(result, rng, smallest, high):
    longest = result.shape.index(max(result.shape))
    spots = []
    for shift in (0, 1):
        where = [jax.random.randint(jax.random.fold_in(rng, axis), (), 0, length) for axis, length in enumerate(result.shape)]
        where[longest] = (where[longest] + shift) % result.shape[longest]
        spots.append(tuple(where))
    return result.at[spots[0]].set(smallest).at[spots[1]].set(high)


def levels(own_key, shape, shards, least, largest):
    factor_of, own = 1.0, jax.random.fold_in(own_key, 6)
    for dim, blocks in shards:
        draws = jnp.exp(jax.random.uniform(jax.random.fold_in(own, dim), (blocks,), jnp.float32, least / len(shards), largest / len(shards)))
        factor_of = factor_of * jnp.repeat(draws, shape[dim] // blocks).reshape([-1 if axis == dim else 1 for axis in range(len(shape))])
    return factor_of


def gaussian(key, extent, spread, reach, split=(), kind=jnp.bfloat16):
    loudness = levels(key, extent, split, -0.22, 0.18) if split else 1.0
    values = jax.random.normal(key, extent, jnp.float32) * spread * loudness
    return jnp.minimum(jnp.maximum(values, -reach), reach).astype(kind)


def setup_inputs(seed: int = 0) -> dict:
    seeds = jax.random.split(jax.random.key(seed), 9)
    resid_in = gaussian(seeds[0], (LAYERS, TOKENS, D), 1.0, 6.0, ((0, 2), (2, 16)))
    mlp_out = gaussian(seeds[1], (LAYERS, TOKENS, D), 1.0, 6.0, ((0, 2), (2, 16)))
    enc_weight = gaussian(seeds[2], (LAYERS, D, LATENTS), D ** -0.5, 0.125, ((0, 2), (2, 16)))
    enc_bias = gaussian(seeds[3], (LAYERS, LATENTS), 0.5, 3.0, ((0, 2), (1, 16)), jnp.float32)
    thresholds = with_ends(jax.random.randint(seeds[4], (LAYERS, LATENTS), 0, 4), jax.random.fold_in(seeds[4], 1), 0, 3).astype(jnp.int32)
    same_dec = gaussian(seeds[5], (LAYERS, LATENTS, D), LATENTS ** -0.5, 0.1875, ((0, 2), (1, 16)))
    next_dec = gaussian(seeds[6], (2, LATENTS, D), LATENTS ** -0.5, 0.1875, ((0, 2), (1, 16)))
    cross_dec = gaussian(seeds[7], (2, 2, LATENTS, D), LATENTS ** -0.5, 0.1875, ((0, 2), (2, 16)))
    return {"resid_in": resid_in, "mlp_out": mlp_out, "enc_weight": enc_weight, "enc_bias": enc_bias, "thresholds": thresholds, "same_dec": same_dec, "next_dec": next_dec, "cross_dec": cross_dec}


jump_width = 0.1


def reference(resid_in, mlp_out, enc_weight, enc_bias, thresholds, same_dec, next_dec, cross_dec):
    pre_acts = []
    gates = []
    activations = []
    for layer in range(4):
        pre = jnp.dot(resid_in[layer], enc_weight[layer], preferred_element_type=jnp.float32) + enc_bias[layer][None, :]
        cut_level = 0.25 * thresholds[layer].astype(jnp.float32)
        gate = jax.nn.sigmoid((pre - cut_level[None, :]) / jump_width)
        pre_acts.append(pre)
        gates.append(gate)
        activations.append((pre * gate).astype(jnp.bfloat16))

    def forward(act, weights):
        return jnp.dot(act, weights, preferred_element_type=jnp.float32)

    rebuilt = [
        forward(activations[0], same_dec[0]),
        forward(activations[1], same_dec[1]) + forward(activations[0], next_dec[0]),
        forward(activations[2], same_dec[2]) + forward(activations[0], cross_dec[0, 0]) + forward(activations[1], cross_dec[0, 1]),
        forward(activations[3], same_dec[3]) + forward(activations[2], next_dec[1]) + forward(activations[0], cross_dec[1, 0]) + forward(activations[1], cross_dec[1, 1]),
    ]
    misfits = [rebuilt[layer] - mlp_out[layer].astype(jnp.float32) for layer in range(4)]
    stacked = jnp.stack(misfits)
    mean_square = jnp.sum(stacked * stacked) / (4.0 * TOKENS * D)
    grads_out = [item.astype(jnp.bfloat16) for item in misfits]

    def backward(grad, weights):
        return jnp.dot(grad, weights.T, preferred_element_type=jnp.float32)

    act_grads = [
        backward(grads_out[0], same_dec[0]) + backward(grads_out[1], next_dec[0]) + backward(grads_out[2], cross_dec[0, 0]) + backward(grads_out[3], cross_dec[1, 0]),
        backward(grads_out[1], same_dec[1]) + backward(grads_out[2], cross_dec[0, 1]) + backward(grads_out[3], cross_dec[1, 1]),
        backward(grads_out[2], same_dec[2]) + backward(grads_out[3], next_dec[1]),
        backward(grads_out[3], same_dec[3]),
    ]

    def outer(act, grad):
        return jnp.dot(act.T, grad, preferred_element_type=jnp.float32)

    grad_enc = []
    grad_bias = []
    for layer in range(4):
        gate = gates[layer]
        pre_grad = act_grads[layer] * (gate + pre_acts[layer] * gate * (1.0 - gate) / jump_width)
        grad_bias.append(jnp.sum(pre_grad, axis=0))
        grad_enc.append(outer(resid_in[layer], pre_grad.astype(jnp.bfloat16)))
    grad_same = [outer(activations[layer], grads_out[layer]) for layer in range(4)]
    grad_next = [outer(activations[0], grads_out[1]), outer(activations[2], grads_out[3])]
    grad_cross = [[outer(activations[0], grads_out[2]), outer(activations[1], grads_out[2])],
                  [outer(activations[0], grads_out[3]), outer(activations[1], grads_out[3])]]
    return (mean_square,
            jnp.stack(grad_enc).astype(jnp.bfloat16),
            jnp.stack(grad_bias),
            jnp.stack(grad_same).astype(jnp.bfloat16),
            jnp.stack(grad_next).astype(jnp.bfloat16),
            jnp.stack([jnp.stack(grad_cross[0]), jnp.stack(grad_cross[1])]).astype(jnp.bfloat16))
```

```python
import functools

import jax
import jax.numpy as jnp
from jax import lax
from jax.experimental import pallas as pl
from jax.experimental.pallas import tpu as pltpu
from jax.sharding import PartitionSpec as P

jump_width = 0.1

Z_STEP, Y_STEP, C_STEP = 4, 2, 1

VMEM = pl.BlockSpec(memory_space=pltpu.VMEM)


def dot_nt(a, b):
    return lax.dot_general(a, b, (((1,), (1,)), ((), ())), preferred_element_type=jnp.float32)


def dot_tn(a, b):
    return lax.dot_general(a, b, (((0,), (0,)), ((), ())), preferred_element_type=jnp.float32)


def dot_nn(a, b):
    return lax.dot_general(a, b, (((1,), (0,)), ((), ())), preferred_element_type=jnp.float32)


def place():
    lat = lax.axis_index("lat")
    return lat // Z_STEP, (lat // Y_STEP) % 2, lat % 2


def lanes(start, size):
    return pl.ds(pl.multiple_of(start, 128), size)


def run(kernel, name, outs, *operands, cost=(0, 0)):
    return pl.pallas_call(
        kernel,
        name=name,
        out_shape=[jax.ShapeDtypeStruct(shape, dtype) for shape, dtype in outs],
        in_specs=[VMEM] * len(operands),
        out_specs=[VMEM] * len(outs),
        compiler_params=pltpu.CompilerParams(vmem_limit_bytes=48 * 1024 * 1024),
        cost_estimate=pl.CostEstimate(flops=cost[0], bytes_accessed=cost[1], transcendentals=0),
    )(*operands)


def to_lat(value, step):
    return lax.ppermute(value, "lat", [(source, source ^ step) for source in range(lax.axis_size("lat"))])


def to_both(value, sec_pairs, step):
    count = lax.axis_size("lat")
    pairs = [(a * count + lat, b * count + (lat ^ step)) for a, b in sec_pairs for lat in range(count)]
    return lax.ppermute(value, ("sec", "lat"), pairs)


DOWN, UP, SWAP = [(0, 1)], [(1, 0)], [(0, 1), (1, 0)]


def pack_kernel(same, nxt, cross, own_s, own_x, far_s, far_x):
    _, y, _ = place()
    sources = [(same.at[1], 0), (nxt.at[0], 1), (same.at[0], 2)]
    width = own_s.shape[1] // 4
    for z in range(4):
        to = slice(z * width, (z + 1) * width)
        for half, (plain, crossed) in enumerate(((own_s, own_x), (far_s, far_x))):
            cols = lanes(z * 2 * width + (y + half) % 2 * width, width)
            for source, row in sources:
                plain[row * 64 : row * 64 + 64, to] = source[:, cols]
            for j in range(2):
                crossed[j * 64 : j * 64 + 64, to] = cross[0, j, :, cols]


def encode_kernel(*refs):
    pieces, (weight, bias, cut, full, slope, act) = refs[:8], refs[8:]
    z, y, c = place()
    block = pieces[0].shape[-1]
    for k in range(4):
        for core in range(2):
            for j in range(2):
                home = (z ^ k) * Z_STEP + (y ^ j) * Y_STEP + (c ^ core)
                for layer in range(2):
                    full[layer, :, lanes(home * block, block)] = pieces[core * 4 + k][j, layer]
    for layer in range(2):
        pre = dot_nt(weight[layer], full[layer]) + bias[layer]
        gate = jax.nn.sigmoid((pre - cut[layer]) / jump_width)
        act[layer] = (pre * gate).astype(jnp.bfloat16)
        slope[layer] = gate + pre * gate * (1.0 - gate) / jump_width


def decode_kernel(act, act_y, act_x, act_d, own_s, own_x, peer_s, peer_x, near_x, diag_x, send, keep):
    _, _, c = place()
    rows = lambda ref: ref.reshape(128, 128)
    first = dot_tn(jnp.concatenate([act[0], act_y[0]]), jnp.concatenate([own_s[128:192], peer_s[128:192]]))
    first += dot_tn(rows(act_x[...]), near_x[...])
    first += dot_tn(rows(act_d[...]), diag_x[...])
    second = dot_tn(jnp.concatenate([act[1], act[0]]), own_s[0:128])
    second += dot_tn(jnp.concatenate([act_y[1], act_y[0]]), peer_s[0:128])
    second += dot_tn(rows(act_x[...]), own_x[...])
    second += dot_tn(rows(act_d[...]), peer_x[...])
    block = send.shape[-1]
    for layer, total in enumerate((first, second)):
        for z in range(4):
            low = total[:, z * 2 * block : z * 2 * block + block]
            high = total[:, z * 2 * block + block : (z + 1) * 2 * block]
            keep[z, layer] = jnp.where(c == 0, low, high)
            send[z, layer] = jnp.where(c == 0, high, low).astype(jnp.bfloat16)


def fold_kernel(keep, got, mine, s1, s2, s3):
    z, _, _ = place()
    mine[...] = keep[z] + got[z].astype(jnp.float32)
    for k, out in ((1, s1), (2, s2), (3, s3)):
        out[...] = (keep[z ^ k] + got[z ^ k].astype(jnp.float32)).astype(jnp.bfloat16)


def misfit_kernel(mine, g1, g2, g3, target, dy):
    total = mine[...] + g1[...].astype(jnp.float32) + g2[...].astype(jnp.float32) + g3[...].astype(jnp.float32)
    dy[...] = (total - target[...].astype(jnp.float32)).astype(jnp.bfloat16)


def act_grad_kernel(mine, core, own_s, own_x, peer_s, peer_x, near_x, diag_x, half, grad_own, to_y, to_x, to_d):
    z, _, c = place()
    block = mine.shape[-1]
    for k in range(4):
        for layer in range(2):
            half[layer, :, lanes(((z ^ k) * 2 + c) * block, block)] = mine[k, layer]
            half[layer, :, lanes(((z ^ k) * 2 + 1 - c) * block, block)] = core[k, layer]
    first, second = half[0], half[1]
    a = dot_nt(own_s[0:128], second)
    grad_own[0] = a[64:128] + dot_nt(own_s[128:192], first)
    grad_own[1] = a[0:64]
    a = dot_nt(peer_s[0:128], second)
    to_y[0:64] = (a[64:128] + dot_nt(peer_s[128:192], first)).astype(jnp.bfloat16)
    to_y[64:128] = a[0:64].astype(jnp.bfloat16)
    to_x[0:128] = (dot_nt(own_x[...], second) + dot_nt(near_x[...], first)).astype(jnp.bfloat16)
    to_d[0:128] = (dot_nt(peer_x[...], second) + dot_nt(diag_x[...], first)).astype(jnp.bfloat16)
    wide = half[...].astype(jnp.float32)
    squares = jnp.sum((wide * wide).reshape(-1, 8, wide.shape[-1]), axis=0)
    part = sum(squares[:, n * 128 : n * 128 + 128] for n in range(squares.shape[1] // 128))
    high = part.astype(jnp.bfloat16)
    low = (part - high.astype(jnp.float32)).astype(jnp.bfloat16)
    for out in (to_y, to_x, to_d):
        out[128:144] = jnp.concatenate([high, low])
    grad_own[2, 0:8] = part


def encoder_grad_kernel(entries, grad_own, from_y, from_x, from_d, slope, full, mean_square, grad_enc, grad_bias):
    leading = lax.axis_index("sec") == 0
    wide = [ref[...].astype(jnp.float32) for ref in (from_y, from_x, from_d)]
    squares = grad_own[2, 0:8] + sum(part[128:136] + part[136:144] for part in wide)
    mean_square[...] = jnp.sum(squares, keepdims=True) / entries
    for layer in range(2):
        rows = slice(layer * 64, layer * 64 + 64)
        across = wide[1][rows] + wide[2][rows]
        total = grad_own[layer] + wide[0][rows] + jnp.where(leading, across, jnp.zeros_like(across))
        pre_grad = total * slope[layer]
        grad_bias[layer : layer + 1] = jnp.sum(pre_grad.T, axis=0, keepdims=True)
        grad_enc[layer] = dot_nn(pre_grad.astype(jnp.bfloat16), full[layer]).astype(jnp.bfloat16)


def decoder_grad_kernel(act, act_x, half, far, far_core, x_own, x_core, d_own, d_core, grad_same, grad_next, grad_cross, dy, dx):
    z, y, c = place()
    leading = lax.axis_index("sec") == 0
    block = far.shape[-1]
    for layer in range(2):
        for n in range(4):
            dy[layer, :, lanes((n * 2 + y) * 2 * block, 2 * block)] = half[layer, :, n * 2 * block : (n + 1) * 2 * block]
        for k in range(4):
            home = (z ^ k) * Z_STEP + (1 - y) * Y_STEP
            dy[layer, :, lanes((home + c) * block, block)] = far[k, layer]
            dy[layer, :, lanes((home + 1 - c) * block, block)] = far_core[k, layer]
    both = jnp.concatenate([act[0], act[1]])
    grad_same[0] = dot_nn(act[0], dy[0]).astype(jnp.bfloat16)
    second = dot_nn(both, dy[1]).astype(jnp.bfloat16)
    grad_next[0] = second[0:64]
    grad_same[1] = second[64:128]

    @pl.when(leading)
    def _():
        for k in range(4):
            for row, own, core in ((y, x_own, x_core), (1 - y, d_own, d_core)):
                home = (z ^ k) * Z_STEP + row * Y_STEP
                dx[:, lanes((home + c) * block, block)] = own[k]
                dx[:, lanes((home + 1 - c) * block, block)] = core[k]
        grad_cross[0] = dot_nn(both, dx[...]).astype(jnp.bfloat16).reshape(2, 64, -1)

    @pl.when(jnp.logical_not(leading))
    def _():
        grad_cross[0] = dot_nn(act_x[...].reshape(128, 128), dy[1]).astype(jnp.bfloat16).reshape(2, 64, -1)


def staged(resid_in, mlp_out, enc_weight, enc_bias, thresholds, same_dec, next_dec, cross_dec):
    bf16, f32 = jnp.bfloat16, jnp.float32
    depth = same_dec.shape[-1]
    block = resid_in.shape[-1]
    entries = 2.0 * resid_in.size * lax.axis_size("lat")
    tall = jnp.swapaxes(enc_weight, 1, 2)
    bias = jnp.broadcast_to(enc_bias[:, :, None], (2, 64, 128))
    cut = jnp.broadcast_to(0.25 * thresholds.astype(f32)[:, :, None], (2, 64, 128))

    other = to_lat(resid_in, Y_STEP)
    own_s, own_x, far_s, far_x = run(
        pack_kernel, "pack",
        [((192, depth // 2), bf16), ((128, depth // 2), bf16)] * 2,
        same_dec, next_dec, cross_dec,
    )
    near = jnp.stack([resid_in, other])
    line = [near] + [to_lat(near, k * Z_STEP) for k in (1, 2, 3)]
    own_s, own_x, far_s, far_x, _ = lax.optimization_barrier((own_s, own_x, far_s, far_x, other))
    peer_s = to_lat(far_s, Y_STEP)
    near_x = to_both(own_x, DOWN, 0)
    peer_x = to_both(far_x, [(1, 1)], Y_STEP)
    diag_x = to_both(far_x, DOWN, Y_STEP)
    pieces = line + [to_lat(piece, C_STEP) for piece in line]
    full, slope, act = run(
        encode_kernel, "encode",
        [((2, 128, depth), bf16), ((2, 64, 128), f32), ((2, 64, 128), bf16)],
        *pieces, tall, bias, cut,
    )
    act_y = to_lat(act, Y_STEP)
    act_x = to_both(act, DOWN, 0)
    act_d = to_both(act, DOWN, Y_STEP)
    send, keep = run(
        decode_kernel, "decode",
        [((4, 2, 128, block), bf16), ((4, 2, 128, block), f32)],
        act, act_y, act_x, act_d, own_s, own_x, peer_s, peer_x, near_x, diag_x,
    )
    got = to_lat(send, C_STEP)
    mine, *parts = run(
        fold_kernel, "fold",
        [((2, 128, block), f32)] + [((2, 128, block), bf16)] * 3,
        keep, got,
    )
    parts = [to_lat(part, k * Z_STEP) for k, part in zip((1, 2, 3), parts)]
    (dy,) = run(misfit_kernel, "misfit", [((2, 128, block), bf16)], mine, *parts, mlp_out)
    row = jnp.stack([dy] + [to_lat(dy, k * Z_STEP) for k in (1, 2, 3)])
    row_core = to_lat(row, C_STEP)
    far = to_lat(row, Y_STEP)
    x_own = to_both(row[:, 0], UP, 0)
    d_own = to_both(row[:, 0], UP, Y_STEP)
    half, grad_own, to_y, to_x, to_d = run(
        act_grad_kernel, "act_grad",
        [((2, 128, depth // 2), bf16), ((3, 64, 128), f32)] + [((144, 128), bf16)] * 3,
        row, row_core, own_s, own_x, peer_s, peer_x, near_x, diag_x,
    )
    from_y = to_lat(to_y, Y_STEP)
    from_x = to_both(to_x, SWAP, 0)
    from_d = to_both(to_d, SWAP, Y_STEP)
    mean_square, grad_enc, grad_bias = run(
        functools.partial(encoder_grad_kernel, entries), "encoder_grad",
        [((1, 1), f32), ((2, 64, depth), bf16), ((2, 64), f32)],
        grad_own, from_y, from_x, from_d, slope, full,
    )
    far_core = to_lat(far, C_STEP)
    x_core = to_lat(x_own, C_STEP)
    d_core = to_lat(d_own, C_STEP)
    operands = (act, act_x, half, far, far_core, x_own, x_core, d_own, d_core)
    outs = [((2, 64, depth), bf16), ((1, 64, depth), bf16), ((1, 2, 64, depth), bf16)]
    grad_same, grad_next, grad_cross = pl.pallas_call(
        decoder_grad_kernel,
        name="decoder_grad",
        out_shape=[jax.ShapeDtypeStruct(shape, dtype) for shape, dtype in outs],
        in_specs=[VMEM] * len(operands),
        out_specs=[VMEM] * len(outs),
        scratch_shapes=[pltpu.VMEM((2, 128, depth), bf16), pltpu.VMEM((128, depth), bf16)],
        compiler_params=pltpu.CompilerParams(vmem_limit_bytes=48 * 1024 * 1024),
    )(*operands)
    return (mean_square[0, 0], jnp.swapaxes(grad_enc, 1, 2), grad_bias, grad_same, grad_next, grad_cross)


def shifted(value, axis, steps):
    count = lax.axis_size(axis)
    first, last = (max(0, -steps), min(count, count - steps))
    return lax.ppermute(value, axis, [(source, source + steps) for source in range(first, last)])


def back_dot(grad, weights):
    return lax.dot_general(
        grad, weights, (((1,), (1,)), ((), ())), preferred_element_type=jnp.float32
    )


def outer_dot(act, grad):
    return lax.dot_general(act, grad, (((0,), (0,)), ((), ())), preferred_element_type=jnp.float32)


def plain(resid_in, mlp_out, enc_weight, enc_bias, thresholds, same_dec, next_dec, cross_dec):
    leading = lax.axis_index("sec") == 0
    inputs_full = lax.all_gather(resid_in, "lat", axis=2, tiled=True)
    pre_act = (
        jnp.einsum("ktd,kdc->ktc", inputs_full, enc_weight, preferred_element_type=jnp.float32)
        + enc_bias[:, None, :]
    )
    cut_level = 0.25 * thresholds.astype(jnp.float32)[:, None, :]
    gate_value = jax.nn.sigmoid((pre_act - cut_level) / jump_width)
    latent_act = (pre_act * gate_value).astype(jnp.bfloat16)
    rebuilt_first = jnp.dot(latent_act[0], same_dec[0], preferred_element_type=jnp.float32)
    rebuilt_second = jnp.dot(
        latent_act[1], same_dec[1], preferred_element_type=jnp.float32
    ) + jnp.dot(latent_act[0], next_dec[0], preferred_element_type=jnp.float32)
    far_weight = shifted(cross_dec, "sec", -1)
    source_act = jnp.where(leading, latent_act, jnp.zeros_like(latent_act))
    near_part = jnp.einsum(
        "ktc,kcd->td", source_act, cross_dec[0], preferred_element_type=jnp.float32
    )
    far_part = jnp.einsum(
        "ktc,kcd->td", source_act, far_weight[0], preferred_element_type=jnp.float32
    )
    partials = jnp.stack([rebuilt_first, rebuilt_second, near_part, far_part])
    summed = lax.psum_scatter(partials, "lat", scatter_dimension=2, tiled=True)
    crossing = shifted(summed[2:], "sec", 1)
    rebuilt = summed[:2] + crossing
    misfit = rebuilt - mlp_out.astype(jnp.float32)
    squared_total = lax.psum(jnp.sum(misfit * misfit), ("sec", "lat"))
    mean_square = squared_total / (2.0 * mlp_out.size * lax.axis_size("lat"))
    dy_rows = misfit.astype(jnp.bfloat16)
    extra_rows = shifted(dy_rows, "sec", -1)
    grad_full = lax.all_gather(
        jnp.concatenate([dy_rows, extra_rows], axis=0), "lat", axis=2, tiled=True
    )
    act_grad = jnp.stack(
        [
            back_dot(grad_full[0], same_dec[0]) + back_dot(grad_full[1], next_dec[0]),
            back_dot(grad_full[1], same_dec[1]),
        ]
    )
    cross_grad = jnp.einsum(
        "td,kcd->ktc", grad_full[2], cross_dec[0], preferred_element_type=jnp.float32
    )
    cross_grad = cross_grad + jnp.einsum(
        "td,kcd->ktc", grad_full[3], far_weight[0], preferred_element_type=jnp.float32
    )
    act_grad = act_grad + cross_grad
    gate_slope = gate_value + pre_act * gate_value * (1.0 - gate_value) / jump_width
    pre_grad = act_grad * gate_slope
    grad_bias = jnp.sum(pre_grad, axis=1)
    pre_rounded = pre_grad.astype(jnp.bfloat16)
    grad_enc = jnp.einsum(
        "ktd,ktc->kdc", inputs_full, pre_rounded, preferred_element_type=jnp.float32
    ).astype(jnp.bfloat16)
    grad_same = jnp.stack(
        [outer_dot(latent_act[0], grad_full[0]), outer_dot(latent_act[1], grad_full[1])]
    ).astype(jnp.bfloat16)
    grad_next = outer_dot(latent_act[0], grad_full[1])[None].astype(jnp.bfloat16)
    near_grad = jnp.einsum(
        "ktc,td->kcd", source_act, grad_full[2], preferred_element_type=jnp.float32
    ).astype(jnp.bfloat16)
    far_grad = jnp.einsum(
        "ktc,td->kcd", source_act, grad_full[3], preferred_element_type=jnp.float32
    ).astype(jnp.bfloat16)
    far_back = shifted(far_grad, "sec", 1)
    grad_cross = jnp.where(leading, near_grad, far_back)[None]
    return (mean_square, grad_enc, grad_bias, grad_same, grad_next, grad_cross)


def solution(mesh):
    body = staged if mesh.shape["lat"] == 16 else plain
    in_specs = (
        P("sec", None, "lat"),
        P("sec", None, "lat"),
        P("sec", None, "lat"),
        P("sec", "lat"),
        P("sec", "lat"),
        P("sec", "lat", None),
        P("sec", "lat", None),
        P("sec", None, "lat", None),
    )
    out_specs = (
        P(),
        P("sec", None, "lat"),
        P("sec", "lat"),
        P("sec", "lat", None),
        P("sec", "lat", None),
        P("sec", None, "lat", None),
    )
    return jax.shard_map(body, mesh=mesh, in_specs=in_specs, out_specs=out_specs, check_vma=False)
```

```python
import functools

import jax
import jax.numpy as jnp
from jax import lax
from jax.experimental import pallas as pl
from jax.experimental.pallas import tpu as pltpu
from jax.sharding import PartitionSpec as P

jump_width = 0.1

Z_STEP, Y_STEP, C_STEP = 4, 2, 1

VMEM = pl.BlockSpec(memory_space=pltpu.VMEM)


def dot_nt(a, b):
    return lax.dot_general(a, b, (((1,), (1,)), ((), ())), preferred_element_type=jnp.float32)


def dot_tn(a, b):
    return lax.dot_general(a, b, (((0,), (0,)), ((), ())), preferred_element_type=jnp.float32)


def dot_nn(a, b):
    return lax.dot_general(a, b, (((1,), (0,)), ((), ())), preferred_element_type=jnp.float32)


def place():
    lat = lax.axis_index("lat")
    return lat // Z_STEP, (lat // Y_STEP) % 2, lat % 2


def lanes(start, size):
    return pl.ds(pl.multiple_of(start, 128), size)


def run(kernel, name, outs, *operands, cost=(0, 0)):
    return pl.pallas_call(
        kernel,
        name=name,
        out_shape=[jax.ShapeDtypeStruct(shape, dtype) for shape, dtype in outs],
        in_specs=[VMEM] * len(operands),
        out_specs=[VMEM] * len(outs),
        compiler_params=pltpu.CompilerParams(vmem_limit_bytes=48 * 1024 * 1024),
        cost_estimate=pl.CostEstimate(flops=cost[0], bytes_accessed=cost[1], transcendentals=0),
    )(*operands)


def to_lat(value, step):
    return lax.ppermute(value, "lat", [(source, source ^ step) for source in range(lax.axis_size("lat"))])


def to_both(value, sec_pairs, step):
    count = lax.axis_size("lat")
    pairs = [(a * count + lat, b * count + (lat ^ step)) for a, b in sec_pairs for lat in range(count)]
    return lax.ppermute(value, ("sec", "lat"), pairs)


DOWN, UP, SWAP = [(0, 1)], [(1, 0)], [(0, 1), (1, 0)]


def pack_kernel(same, nxt, cross, own_s, own_x, far_s, far_x):
    _, y, _ = place()
    sources = [(same.at[1], 0), (nxt.at[0], 1), (same.at[0], 2)]
    width = own_s.shape[1] // 4
    for z in range(4):
        to = slice(z * width, (z + 1) * width)
        for half, (plain, crossed) in enumerate(((own_s, own_x), (far_s, far_x))):
            cols = lanes(z * 2 * width + (y + half) % 2 * width, width)
            for source, row in sources:
                plain[row * 64 : row * 64 + 64, to] = source[:, cols]
            for j in range(2):
                crossed[j * 64 : j * 64 + 64, to] = cross[0, j, :, cols]


def pair_kernel(own, other, pair):
    pair[0] = own[...]
    pair[1] = other[...]


def row_kernel(own, *refs):
    others, (row, lead) = refs[:3], refs[3:]
    for k, part in enumerate((own, *others)):
        row[k] = part[...]
        lead[k] = part[0]


def encode_kernel(*refs):
    pieces, (weight, bias, cut, full, slope, act) = refs[:8], refs[8:]
    z, y, c = place()
    block = pieces[0].shape[-1]
    for k in range(4):
        for core in range(2):
            for j in range(2):
                home = (z ^ k) * Z_STEP + (y ^ j) * Y_STEP + (c ^ core)
                for layer in range(2):
                    full[layer, :, lanes(home * block, block)] = pieces[core * 4 + k][j, layer]
    for layer in range(2):
        pre = dot_nt(weight[layer], full[layer]) + bias[layer]
        gate = jax.nn.sigmoid((pre - cut[layer]) / jump_width)
        act[layer] = (pre * gate).astype(jnp.bfloat16)
        slope[layer] = gate + pre * gate * (1.0 - gate) / jump_width


def decode_kernel(act, act_y, act_x, act_d, own_s, own_x, peer_s, peer_x, near_x, diag_x, send, keep):
    _, _, c = place()
    rows = lambda ref: ref.reshape(128, 128)
    first = dot_tn(jnp.concatenate([act[0], act_y[0]]), jnp.concatenate([own_s[128:192], peer_s[128:192]]))
    first += dot_tn(rows(act_x[...]), near_x[...])
    first += dot_tn(rows(act_d[...]), diag_x[...])
    second = dot_tn(jnp.concatenate([act[1], act[0]]), own_s[0:128])
    second += dot_tn(jnp.concatenate([act_y[1], act_y[0]]), peer_s[0:128])
    second += dot_tn(rows(act_x[...]), own_x[...])
    second += dot_tn(rows(act_d[...]), peer_x[...])
    block = send.shape[-1]
    for layer, total in enumerate((first, second)):
        for z in range(4):
            low = total[:, z * 2 * block : z * 2 * block + block]
            high = total[:, z * 2 * block + block : (z + 1) * 2 * block]
            keep[z, layer] = jnp.where(c == 0, low, high)
            send[z, layer] = jnp.where(c == 0, high, low).astype(jnp.bfloat16)


def fold_kernel(keep, got, mine, s1, s2, s3):
    z, _, _ = place()
    mine[...] = keep[z] + got[z].astype(jnp.float32)
    for k, out in ((1, s1), (2, s2), (3, s3)):
        out[...] = (keep[z ^ k] + got[z ^ k].astype(jnp.float32)).astype(jnp.bfloat16)


def misfit_kernel(mine, g1, g2, g3, target, dy):
    total = mine[...] + g1[...].astype(jnp.float32) + g2[...].astype(jnp.float32) + g3[...].astype(jnp.float32)
    dy[...] = (total - target[...].astype(jnp.float32)).astype(jnp.bfloat16)


def act_grad_kernel(mine, core, own_s, own_x, peer_s, peer_x, near_x, diag_x, half, grad_own, to_y, to_x, to_d):
    z, _, c = place()
    block = mine.shape[-1]
    for k in range(4):
        for layer in range(2):
            half[layer, :, lanes(((z ^ k) * 2 + c) * block, block)] = mine[k, layer]
            half[layer, :, lanes(((z ^ k) * 2 + 1 - c) * block, block)] = core[k, layer]
    first, second = half[0], half[1]
    a = dot_nt(own_s[0:128], second)
    grad_own[0] = a[64:128] + dot_nt(own_s[128:192], first)
    grad_own[1] = a[0:64]
    a = dot_nt(peer_s[0:128], second)
    to_y[0:64] = (a[64:128] + dot_nt(peer_s[128:192], first)).astype(jnp.bfloat16)
    to_y[64:128] = a[0:64].astype(jnp.bfloat16)
    to_x[0:128] = (dot_nt(own_x[...], second) + dot_nt(near_x[...], first)).astype(jnp.bfloat16)
    to_d[0:128] = (dot_nt(peer_x[...], second) + dot_nt(diag_x[...], first)).astype(jnp.bfloat16)
    wide = half[...].astype(jnp.float32)
    squares = jnp.sum((wide * wide).reshape(-1, 8, wide.shape[-1]), axis=0)
    part = sum(squares[:, n * 128 : n * 128 + 128] for n in range(squares.shape[1] // 128))
    high = part.astype(jnp.bfloat16)
    low = (part - high.astype(jnp.float32)).astype(jnp.bfloat16)
    for out in (to_y, to_x, to_d):
        out[128:144] = jnp.concatenate([high, low])
    grad_own[2, 0:8] = part


def encoder_grad_kernel(entries, grad_own, from_y, from_x, from_d, slope, full, mean_square, grad_enc, grad_bias):
    leading = lax.axis_index("sec") == 0
    wide = [ref[...].astype(jnp.float32) for ref in (from_y, from_x, from_d)]
    squares = grad_own[2, 0:8] + sum(part[128:136] + part[136:144] for part in wide)
    mean_square[...] = jnp.sum(squares, keepdims=True) / entries
    for layer in range(2):
        rows = slice(layer * 64, layer * 64 + 64)
        across = wide[1][rows] + wide[2][rows]
        total = grad_own[layer] + wide[0][rows] + jnp.where(leading, across, jnp.zeros_like(across))
        pre_grad = total * slope[layer]
        grad_bias[layer : layer + 1] = jnp.sum(pre_grad.T, axis=0, keepdims=True)
        grad_enc[layer] = dot_nn(pre_grad.astype(jnp.bfloat16), full[layer]).astype(jnp.bfloat16)


def decoder_grad_kernel(act, act_x, half, far, far_core, x_own, x_core, d_own, d_core, grad_same, grad_next, grad_cross, dy, dx):
    z, y, c = place()
    leading = lax.axis_index("sec") == 0
    block = far.shape[-1]
    for layer in range(2):
        for n in range(4):
            dy[layer, :, lanes((n * 2 + y) * 2 * block, 2 * block)] = half[layer, :, n * 2 * block : (n + 1) * 2 * block]
        for k in range(4):
            home = (z ^ k) * Z_STEP + (1 - y) * Y_STEP
            dy[layer, :, lanes((home + c) * block, block)] = far[k, layer]
            dy[layer, :, lanes((home + 1 - c) * block, block)] = far_core[k, layer]
    both = jnp.concatenate([act[0], act[1]])
    grad_same[0] = dot_nn(act[0], dy[0]).astype(jnp.bfloat16)
    second = dot_nn(both, dy[1]).astype(jnp.bfloat16)
    grad_next[0] = second[0:64]
    grad_same[1] = second[64:128]

    @pl.when(leading)
    def _():
        for k in range(4):
            for row, own, core in ((y, x_own, x_core), (1 - y, d_own, d_core)):
                home = (z ^ k) * Z_STEP + row * Y_STEP
                dx[:, lanes((home + c) * block, block)] = own[k]
                dx[:, lanes((home + 1 - c) * block, block)] = core[k]
        grad_cross[0] = dot_nn(both, dx[...]).astype(jnp.bfloat16).reshape(2, 64, -1)

    @pl.when(jnp.logical_not(leading))
    def _():
        grad_cross[0] = dot_nn(act_x[...].reshape(128, 128), dy[1]).astype(jnp.bfloat16).reshape(2, 64, -1)


def staged(resid_in, mlp_out, enc_weight, enc_bias, thresholds, same_dec, next_dec, cross_dec):
    bf16, f32 = jnp.bfloat16, jnp.float32
    depth = same_dec.shape[-1]
    block = resid_in.shape[-1]
    entries = 2.0 * resid_in.size * lax.axis_size("lat")
    tall = jnp.swapaxes(enc_weight, 1, 2)
    bias = jnp.broadcast_to(enc_bias[:, :, None], (2, 64, 128))
    cut = jnp.broadcast_to(0.25 * thresholds.astype(f32)[:, :, None], (2, 64, 128))

    other = to_lat(resid_in, Y_STEP)
    own_s, own_x, far_s, far_x = run(
        pack_kernel, "pack",
        [((192, depth // 2), bf16), ((128, depth // 2), bf16)] * 2,
        same_dec, next_dec, cross_dec,
    )
    far_s, far_x, lead_x, other = lax.optimization_barrier((far_s, far_x, own_x, other))
    (near,) = run(pair_kernel, "pair", [((2, 2, 128, block), bf16)], resid_in, other)
    line = [near] + [to_lat(near, k * Z_STEP) for k in (1, 2, 3)]
    peer_x = to_lat(far_x, Y_STEP)
    near_x = to_both(lead_x, SWAP, 0)
    peer_s = to_lat(far_s, Y_STEP)
    diag_x = to_both(peer_x, SWAP, 0)
    pieces = line + [to_lat(piece, C_STEP) for piece in line]
    full, slope, act = run(
        encode_kernel, "encode",
        [((2, 128, depth), bf16), ((2, 64, 128), f32), ((2, 64, 128), bf16)],
        *pieces, tall, bias, cut,
    )
    act_y = to_lat(act, Y_STEP)
    act_x = to_both(act, DOWN, 0)
    act_d = to_both(act, DOWN, Y_STEP)
    send, keep = run(
        decode_kernel, "decode",
        [((4, 2, 128, block), bf16), ((4, 2, 128, block), f32)],
        act, act_y, act_x, act_d, own_s, own_x, peer_s, peer_x, near_x, diag_x,
    )
    got = to_lat(send, C_STEP)
    mine, *parts = run(
        fold_kernel, "fold",
        [((2, 128, block), f32)] + [((2, 128, block), bf16)] * 3,
        keep, got,
    )
    parts = [to_lat(part, k * Z_STEP) for k, part in zip((1, 2, 3), parts)]
    (dy,) = run(misfit_kernel, "misfit", [((2, 128, block), bf16)], mine, *parts, mlp_out)
    row, lead = run(
        row_kernel, "row",
        [((4, 2, 128, block), bf16), ((4, 128, block), bf16)],
        dy, *[to_lat(dy, k * Z_STEP) for k in (1, 2, 3)],
    )
    row_core = to_lat(row, C_STEP)
    far = to_lat(row, Y_STEP)
    x_own = to_both(lead, UP, 0)
    d_own = to_both(lead, UP, Y_STEP)
    half, grad_own, to_y, to_x, to_d = run(
        act_grad_kernel, "act_grad",
        [((2, 128, depth // 2), bf16), ((3, 64, 128), f32)] + [((144, 128), bf16)] * 3,
        row, row_core, own_s, own_x, peer_s, peer_x, near_x, diag_x,
    )
    from_y = to_lat(to_y, Y_STEP)
    from_x = to_both(to_x, SWAP, 0)
    from_d = to_both(to_d, SWAP, Y_STEP)
    mean_square, grad_enc, grad_bias = run(
        functools.partial(encoder_grad_kernel, entries), "encoder_grad",
        [((1, 1), f32), ((2, 64, depth), bf16), ((2, 64), f32)],
        grad_own, from_y, from_x, from_d, slope, full,
    )
    far, x_own, d_own, _, _, _ = lax.optimization_barrier((far, x_own, d_own, from_y, from_x, from_d))
    far_core = to_lat(far, C_STEP)
    x_core = to_lat(x_own, C_STEP)
    d_core = to_lat(d_own, C_STEP)
    operands = (act, act_x, half, far, far_core, x_own, x_core, d_own, d_core)
    outs = [((2, 64, depth), bf16), ((1, 64, depth), bf16), ((1, 2, 64, depth), bf16)]
    grad_same, grad_next, grad_cross = pl.pallas_call(
        decoder_grad_kernel,
        name="decoder_grad",
        out_shape=[jax.ShapeDtypeStruct(shape, dtype) for shape, dtype in outs],
        in_specs=[VMEM] * len(operands),
        out_specs=[VMEM] * len(outs),
        scratch_shapes=[pltpu.VMEM((2, 128, depth), bf16), pltpu.VMEM((128, depth), bf16)],
        compiler_params=pltpu.CompilerParams(vmem_limit_bytes=48 * 1024 * 1024),
    )(*operands)
    return (mean_square[0, 0], jnp.swapaxes(grad_enc, 1, 2), grad_bias, grad_same, grad_next, grad_cross)


def shifted(value, axis, steps):
    count = lax.axis_size(axis)
    first, last = (max(0, -steps), min(count, count - steps))
    return lax.ppermute(value, axis, [(source, source + steps) for source in range(first, last)])


def back_dot(grad, weights):
    return lax.dot_general(
        grad, weights, (((1,), (1,)), ((), ())), preferred_element_type=jnp.float32
    )


def outer_dot(act, grad):
    return lax.dot_general(act, grad, (((0,), (0,)), ((), ())), preferred_element_type=jnp.float32)


def plain(resid_in, mlp_out, enc_weight, enc_bias, thresholds, same_dec, next_dec, cross_dec):
    leading = lax.axis_index("sec") == 0
    inputs_full = lax.all_gather(resid_in, "lat", axis=2, tiled=True)
    pre_act = (
        jnp.einsum("ktd,kdc->ktc", inputs_full, enc_weight, preferred_element_type=jnp.float32)
        + enc_bias[:, None, :]
    )
    cut_level = 0.25 * thresholds.astype(jnp.float32)[:, None, :]
    gate_value = jax.nn.sigmoid((pre_act - cut_level) / jump_width)
    latent_act = (pre_act * gate_value).astype(jnp.bfloat16)
    rebuilt_first = jnp.dot(latent_act[0], same_dec[0], preferred_element_type=jnp.float32)
    rebuilt_second = jnp.dot(
        latent_act[1], same_dec[1], preferred_element_type=jnp.float32
    ) + jnp.dot(latent_act[0], next_dec[0], preferred_element_type=jnp.float32)
    far_weight = shifted(cross_dec, "sec", -1)
    source_act = jnp.where(leading, latent_act, jnp.zeros_like(latent_act))
    near_part = jnp.einsum(
        "ktc,kcd->td", source_act, cross_dec[0], preferred_element_type=jnp.float32
    )
    far_part = jnp.einsum(
        "ktc,kcd->td", source_act, far_weight[0], preferred_element_type=jnp.float32
    )
    partials = jnp.stack([rebuilt_first, rebuilt_second, near_part, far_part])
    summed = lax.psum_scatter(partials, "lat", scatter_dimension=2, tiled=True)
    crossing = shifted(summed[2:], "sec", 1)
    rebuilt = summed[:2] + crossing
    misfit = rebuilt - mlp_out.astype(jnp.float32)
    squared_total = lax.psum(jnp.sum(misfit * misfit), ("sec", "lat"))
    mean_square = squared_total / (2.0 * mlp_out.size * lax.axis_size("lat"))
    dy_rows = misfit.astype(jnp.bfloat16)
    extra_rows = shifted(dy_rows, "sec", -1)
    grad_full = lax.all_gather(
        jnp.concatenate([dy_rows, extra_rows], axis=0), "lat", axis=2, tiled=True
    )
    act_grad = jnp.stack(
        [
            back_dot(grad_full[0], same_dec[0]) + back_dot(grad_full[1], next_dec[0]),
            back_dot(grad_full[1], same_dec[1]),
        ]
    )
    cross_grad = jnp.einsum(
        "td,kcd->ktc", grad_full[2], cross_dec[0], preferred_element_type=jnp.float32
    )
    cross_grad = cross_grad + jnp.einsum(
        "td,kcd->ktc", grad_full[3], far_weight[0], preferred_element_type=jnp.float32
    )
    act_grad = act_grad + cross_grad
    gate_slope = gate_value + pre_act * gate_value * (1.0 - gate_value) / jump_width
    pre_grad = act_grad * gate_slope
    grad_bias = jnp.sum(pre_grad, axis=1)
    pre_rounded = pre_grad.astype(jnp.bfloat16)
    grad_enc = jnp.einsum(
        "ktd,ktc->kdc", inputs_full, pre_rounded, preferred_element_type=jnp.float32
    ).astype(jnp.bfloat16)
    grad_same = jnp.stack(
        [outer_dot(latent_act[0], grad_full[0]), outer_dot(latent_act[1], grad_full[1])]
    ).astype(jnp.bfloat16)
    grad_next = outer_dot(latent_act[0], grad_full[1])[None].astype(jnp.bfloat16)
    near_grad = jnp.einsum(
        "ktc,td->kcd", source_act, grad_full[2], preferred_element_type=jnp.float32
    ).astype(jnp.bfloat16)
    far_grad = jnp.einsum(
        "ktc,td->kcd", source_act, grad_full[3], preferred_element_type=jnp.float32
    ).astype(jnp.bfloat16)
    far_back = shifted(far_grad, "sec", 1)
    grad_cross = jnp.where(leading, near_grad, far_back)[None]
    return (mean_square, grad_enc, grad_bias, grad_same, grad_next, grad_cross)


def solution(mesh):
    body = staged if mesh.shape["lat"] == 16 else plain
    in_specs = (
        P("sec", None, "lat"),
        P("sec", None, "lat"),
        P("sec", None, "lat"),
        P("sec", "lat"),
        P("sec", "lat"),
        P("sec", "lat", None),
        P("sec", "lat", None),
        P("sec", None, "lat", None),
    )
    out_specs = (
        P(),
        P("sec", None, "lat"),
        P("sec", "lat"),
        P("sec", "lat", None),
        P("sec", "lat", None),
        P("sec", None, "lat", None),
    )
    return jax.shard_map(body, mesh=mesh, in_specs=in_specs, out_specs=out_specs, check_vma=False)
```

```python
import functools

import jax
import jax.numpy as jnp
from jax import lax
from jax.experimental import pallas as pl
from jax.experimental.pallas import tpu as pltpu
from jax.sharding import PartitionSpec as P

jump_width = 0.1

Z_STEP, Y_STEP, C_STEP = 4, 2, 1

VMEM = pl.BlockSpec(memory_space=pltpu.VMEM)


def dot_nt(a, b):
    return lax.dot_general(a, b, (((1,), (1,)), ((), ())), preferred_element_type=jnp.float32)


def dot_tn(a, b):
    return lax.dot_general(a, b, (((0,), (0,)), ((), ())), preferred_element_type=jnp.float32)


def dot_nn(a, b):
    return lax.dot_general(a, b, (((1,), (0,)), ((), ())), preferred_element_type=jnp.float32)


def place():
    lat = lax.axis_index("lat")
    return lat // Z_STEP, (lat // Y_STEP) % 2, lat % 2


def lanes(start, size):
    return pl.ds(pl.multiple_of(start, 128), size)


def run(kernel, name, outs, *operands, cost=(0, 0)):
    return pl.pallas_call(
        kernel,
        name=name,
        out_shape=[jax.ShapeDtypeStruct(shape, dtype) for shape, dtype in outs],
        in_specs=[VMEM] * len(operands),
        out_specs=[VMEM] * len(outs),
        compiler_params=pltpu.CompilerParams(vmem_limit_bytes=48 * 1024 * 1024),
        cost_estimate=pl.CostEstimate(flops=cost[0], bytes_accessed=cost[1], transcendentals=0),
    )(*operands)


def to_lat(value, step):
    return lax.ppermute(value, "lat", [(source, source ^ step) for source in range(lax.axis_size("lat"))])


def to_both(value, sec_pairs, step):
    count = lax.axis_size("lat")
    pairs = [(a * count + lat, b * count + (lat ^ step)) for a, b in sec_pairs for lat in range(count)]
    return lax.ppermute(value, ("sec", "lat"), pairs)


SWAP = [(0, 1), (1, 0)]


def pack_kernel(same, nxt, cross, own_s, own_x, far_s, far_x, same_v, nxt_v, cross_v, sems):
    _, y, _ = place()
    width = own_s.shape[-1] // 4
    copies = [
        pltpu.make_async_copy(source, target, sems.at[n])
        for n, (source, target) in enumerate(((cross.at[0], cross_v), (same, same_v), (nxt.at[0], nxt_v)))
    ]
    for copy in copies:
        copy.start()

    def move(source, plain, row, crossed):
        for z in range(4):
            to = slice(z * width, (z + 1) * width)
            for half, out in enumerate((plain, crossed)):
                out[row, :, to] = source[:, lanes(z * 2 * width + (y + half) % 2 * width, width)]

    copies[0].wait()
    for j in range(2):
        move(cross_v.at[j], own_x, j, far_x)
    copies[1].wait()
    for layer in range(2):
        move(same_v.at[layer], own_s, layer, far_s)
    copies[2].wait()
    move(nxt_v, own_s, 2, far_s)


def stacked(ref, first, last):
    return ref[first:last].reshape((last - first) * ref.shape[1], ref.shape[2])


def pair_kernel(own, other, pair):
    pair[0] = own[...]
    pair[1] = other[...]


def row_kernel(own, *refs):
    others, (row, lead) = refs[:3], refs[3:]
    for k, part in enumerate((own, *others)):
        row[k] = part[...]
        lead[k] = part[0]


def encode_kernel(*refs):
    pieces, (weight, bias, cut, full, slope, act) = refs[:10], refs[10:]
    z, y, c = place()
    block = pieces[0].shape[-1]

    def put(k, j, core, layer, value):
        home = (z ^ k) * Z_STEP + (y ^ j) * Y_STEP + (c ^ core)
        full[layer, :, lanes(home * block, block)] = value

    for core in range(2):
        mine, line1, line3, line2, line2_y = pieces[core * 5 : core * 5 + 5]
        for layer in range(2):
            for j in range(2):
                for k, pair in ((0, mine), (1, line1), (3, line3)):
                    put(k, j, core, layer, pair[j, layer])
            put(2, 0, core, layer, line2[layer])
            put(2, 1, core, layer, line2_y[layer])
    for layer in range(2):
        pre = dot_nt(weight[layer], full[layer]) + bias[layer]
        gate = jax.nn.sigmoid((pre - cut[layer]) / jump_width)
        act[layer] = (pre * gate).astype(jnp.bfloat16)
        slope[layer] = gate + pre * gate * (1.0 - gate) / jump_width


def decode_kernel(act, act_y, act_x, act_d, own_s, own_x, peer_s, peer_x, near_x, diag_x, send, keep):
    _, _, c = place()
    leading = lax.axis_index("sec") == 0
    across, diagonal = (
        jnp.where(leading, jnp.zeros((128, 128), jnp.bfloat16), stacked(ref, 0, 2)) for ref in (act_x, act_d)
    )
    first = dot_tn(jnp.concatenate([act[0], act_y[0]]), jnp.concatenate([own_s[0], peer_s[0]]))
    first += dot_tn(across, stacked(near_x, 0, 2))
    first += dot_tn(diagonal, stacked(diag_x, 0, 2))
    second = dot_tn(jnp.concatenate([act[1], act[0]]), stacked(own_s, 1, 3))
    second += dot_tn(jnp.concatenate([act_y[1], act_y[0]]), stacked(peer_s, 1, 3))
    second += dot_tn(across, stacked(own_x, 0, 2))
    second += dot_tn(diagonal, stacked(peer_x, 0, 2))
    block = send.shape[-1]
    for layer, total in enumerate((first, second)):
        for z in range(4):
            low = total[:, z * 2 * block : z * 2 * block + block]
            high = total[:, z * 2 * block + block : (z + 1) * 2 * block]
            keep[z, layer] = jnp.where(c == 0, low, high)
            send[z, layer] = jnp.where(c == 0, high, low).astype(jnp.bfloat16)


def fold_kernel(keep, got, mine, s1, s2, s3):
    z, _, _ = place()
    mine[...] = keep[z] + got[z].astype(jnp.float32)
    for k, out in ((1, s1), (2, s2), (3, s3)):
        out[...] = (keep[z ^ k] + got[z ^ k].astype(jnp.float32)).astype(jnp.bfloat16)


def misfit_kernel(mine, g1, g2, g3, target, dy):
    total = mine[...] + g1[...].astype(jnp.float32) + g2[...].astype(jnp.float32) + g3[...].astype(jnp.float32)
    dy[...] = (total - target[...].astype(jnp.float32)).astype(jnp.bfloat16)


def act_grad_kernel(mine, core, own_s, own_x, peer_s, peer_x, near_x, diag_x, half, grad_own, to_y, to_x, to_d):
    z, _, c = place()
    block = mine.shape[-1]
    for k in range(4):
        for layer in range(2):
            half[layer, :, lanes(((z ^ k) * 2 + c) * block, block)] = mine[k, layer]
            half[layer, :, lanes(((z ^ k) * 2 + 1 - c) * block, block)] = core[k, layer]
    first, second = half[0], half[1]
    a = dot_nt(stacked(own_s, 1, 3), second)
    grad_own[0] = a[64:128] + dot_nt(own_s[0], first)
    grad_own[1] = a[0:64]
    a = dot_nt(stacked(peer_s, 1, 3), second)
    to_y[0:64] = (a[64:128] + dot_nt(peer_s[0], first)).astype(jnp.bfloat16)
    to_y[64:128] = a[0:64].astype(jnp.bfloat16)
    to_x[0:128] = (dot_nt(stacked(own_x, 0, 2), second) + dot_nt(stacked(near_x, 0, 2), first)).astype(jnp.bfloat16)
    to_d[0:128] = (dot_nt(stacked(peer_x, 0, 2), second) + dot_nt(stacked(diag_x, 0, 2), first)).astype(jnp.bfloat16)
    wide = half[...].astype(jnp.float32)
    squares = jnp.sum((wide * wide).reshape(-1, 8, wide.shape[-1]), axis=0)
    part = sum(squares[:, n * 128 : n * 128 + 128] for n in range(squares.shape[1] // 128))
    high = part.astype(jnp.bfloat16)
    low = (part - high.astype(jnp.float32)).astype(jnp.bfloat16)
    for out in (to_y, to_x, to_d):
        out[128:144] = jnp.concatenate([high, low])
    grad_own[2, 0:8] = part


def encoder_grad_kernel(entries, grad_own, from_y, from_x, from_d, slope, full, mean_square, grad_enc, grad_bias):
    leading = lax.axis_index("sec") == 0
    wide = [ref[...].astype(jnp.float32) for ref in (from_y, from_x, from_d)]
    squares = grad_own[2, 0:8] + sum(part[128:136] + part[136:144] for part in wide)
    mean_square[...] = jnp.sum(squares, keepdims=True) / entries
    for layer in range(2):
        rows = slice(layer * 64, layer * 64 + 64)
        across = wide[1][rows] + wide[2][rows]
        total = grad_own[layer] + wide[0][rows] + jnp.where(leading, across, jnp.zeros_like(across))
        pre_grad = total * slope[layer]
        grad_bias[layer : layer + 1] = jnp.sum(pre_grad.T, axis=0, keepdims=True)
        grad_enc[layer] = dot_nn(pre_grad.astype(jnp.bfloat16), full[layer]).astype(jnp.bfloat16)


def decoder_grad_kernel(act, act_x, half, far, far_core, x_own, x_core, d_own, d_core, grad_same, grad_next, grad_cross, dy, dx):
    z, y, c = place()
    leading = lax.axis_index("sec") == 0
    block = far.shape[-1]
    for layer in range(2):
        for n in range(4):
            dy[layer, :, lanes((n * 2 + y) * 2 * block, 2 * block)] = half[layer, :, n * 2 * block : (n + 1) * 2 * block]
        for k in range(4):
            home = (z ^ k) * Z_STEP + (1 - y) * Y_STEP
            dy[layer, :, lanes((home + c) * block, block)] = far[k, layer]
            dy[layer, :, lanes((home + 1 - c) * block, block)] = far_core[k, layer]
    both = jnp.concatenate([act[0], act[1]])
    grad_same[0] = dot_nn(act[0], dy[0]).astype(jnp.bfloat16)
    second = dot_nn(both, dy[1]).astype(jnp.bfloat16)
    grad_next[0] = second[0:64]
    grad_same[1] = second[64:128]

    @pl.when(leading)
    def _():
        for k in range(4):
            for row, own, core in ((y, x_own, x_core), (1 - y, d_own, d_core)):
                home = (z ^ k) * Z_STEP + row * Y_STEP
                dx[:, lanes((home + c) * block, block)] = own[k]
                dx[:, lanes((home + 1 - c) * block, block)] = core[k]
        grad_cross[0] = dot_nn(both, dx[...]).astype(jnp.bfloat16).reshape(2, 64, -1)

    @pl.when(jnp.logical_not(leading))
    def _():
        grad_cross[0] = dot_nn(act_x[...].reshape(128, 128), dy[1]).astype(jnp.bfloat16).reshape(2, 64, -1)


def staged(resid_in, mlp_out, enc_weight, enc_bias, thresholds, same_dec, next_dec, cross_dec):
    bf16, f32 = jnp.bfloat16, jnp.float32
    depth = same_dec.shape[-1]
    block = resid_in.shape[-1]
    entries = 2.0 * resid_in.size * lax.axis_size("lat")
    tall = jnp.swapaxes(enc_weight, 1, 2)
    bias = jnp.broadcast_to(enc_bias[:, :, None], (2, 64, 128))
    cut = jnp.broadcast_to(0.25 * thresholds.astype(f32)[:, :, None], (2, 64, 128))

    other = to_lat(resid_in, Y_STEP)
    line2 = to_lat(resid_in, 2 * Z_STEP)
    shapes = [((3, 64, depth // 2), bf16), ((2, 64, depth // 2), bf16)] * 2
    own_s, own_x, far_s, far_x = pl.pallas_call(
        pack_kernel,
        name="pack",
        out_shape=[jax.ShapeDtypeStruct(shape, dtype) for shape, dtype in shapes],
        in_specs=[pl.BlockSpec(memory_space=pl.ANY)] * 3,
        out_specs=[VMEM] * 4,
        scratch_shapes=[
            pltpu.VMEM((2, 64, depth), bf16),
            pltpu.VMEM((64, depth), bf16),
            pltpu.VMEM((2, 64, depth), bf16),
            pltpu.SemaphoreType.DMA((3,)),
        ],
    )(same_dec, next_dec, cross_dec)
    (near,) = run(pair_kernel, "pair", [((2, 2, 128, block), bf16)], resid_in, other)
    line1, line3 = (to_lat(near, k * Z_STEP) for k in (1, 3))
    line2, far_x, _ = lax.optimization_barrier((line2, far_x, near))
    line2_y = to_lat(line2, Y_STEP)
    peer_x = to_lat(far_x, Y_STEP)
    lead_x, _ = lax.optimization_barrier((own_x, other))
    near_x = to_both(lead_x, SWAP, 0)
    far_s, _, _ = lax.optimization_barrier((far_s, other, line2))
    peer_s = to_lat(far_s, Y_STEP)
    diag_x = to_both(peer_x, SWAP, 0)
    line1, line3, near_x = lax.optimization_barrier((line1, line3, near_x))
    pieces = [near, line1, line3, line2, line2_y]
    pieces += [to_lat(piece, C_STEP) for piece in pieces]
    full, slope, act = run(
        encode_kernel, "encode",
        [((2, 128, depth), bf16), ((2, 64, 128), f32), ((2, 64, 128), bf16)],
        *pieces, tall, bias, cut,
    )
    act_y = to_lat(act, Y_STEP)
    act_x = to_both(act, SWAP, 0)
    act_d = to_both(act, SWAP, Y_STEP)
    send, keep = run(
        decode_kernel, "decode",
        [((4, 2, 128, block), bf16), ((4, 2, 128, block), f32)],
        act, act_y, act_x, act_d, own_s, own_x, peer_s, peer_x, near_x, diag_x,
    )
    got = to_lat(send, C_STEP)
    mine, *parts = run(
        fold_kernel, "fold",
        [((2, 128, block), f32)] + [((2, 128, block), bf16)] * 3,
        keep, got,
    )
    parts = [to_lat(part, k * Z_STEP) for k, part in zip((1, 2, 3), parts)]
    (dy,) = run(misfit_kernel, "misfit", [((2, 128, block), bf16)], mine, *parts, mlp_out)
    row, lead = run(
        row_kernel, "row",
        [((4, 2, 128, block), bf16), ((4, 128, block), bf16)],
        dy, *[to_lat(dy, k * Z_STEP) for k in (1, 2, 3)],
    )
    row_core = to_lat(row, C_STEP)
    far = to_lat(row, Y_STEP)
    x_own = to_both(lead, SWAP, 0)
    d_own = to_both(lead, SWAP, Y_STEP)
    half, grad_own, to_y, to_x, to_d = run(
        act_grad_kernel, "act_grad",
        [((2, 128, depth // 2), bf16), ((3, 64, 128), f32)] + [((144, 128), bf16)] * 3,
        row, row_core, own_s, own_x, peer_s, peer_x, near_x, diag_x,
    )
    from_y = to_lat(to_y, Y_STEP)
    from_x = to_both(to_x, SWAP, 0)
    from_d = to_both(to_d, SWAP, Y_STEP)
    mean_square, grad_enc, grad_bias = run(
        functools.partial(encoder_grad_kernel, entries), "encoder_grad",
        [((1, 1), f32), ((2, 64, depth), bf16), ((2, 64), f32)],
        grad_own, from_y, from_x, from_d, slope, full,
    )
    far, x_own, d_own, _, _, _ = lax.optimization_barrier((far, x_own, d_own, from_y, from_x, from_d))
    far_core = to_lat(far, C_STEP)
    x_core = to_lat(x_own, C_STEP)
    d_core = to_lat(d_own, C_STEP)
    operands = (act, act_x, half, far, far_core, x_own, x_core, d_own, d_core)
    outs = [((2, 64, depth), bf16), ((1, 64, depth), bf16), ((1, 2, 64, depth), bf16)]
    grad_same, grad_next, grad_cross = pl.pallas_call(
        decoder_grad_kernel,
        name="decoder_grad",
        out_shape=[jax.ShapeDtypeStruct(shape, dtype) for shape, dtype in outs],
        in_specs=[VMEM] * len(operands),
        out_specs=[VMEM] * len(outs),
        scratch_shapes=[pltpu.VMEM((2, 128, depth), bf16), pltpu.VMEM((128, depth), bf16)],
        compiler_params=pltpu.CompilerParams(vmem_limit_bytes=48 * 1024 * 1024),
    )(*operands)
    return (mean_square[0, 0], jnp.swapaxes(grad_enc, 1, 2), grad_bias, grad_same, grad_next, grad_cross)


def shifted(value, axis, steps):
    count = lax.axis_size(axis)
    first, last = (max(0, -steps), min(count, count - steps))
    return lax.ppermute(value, axis, [(source, source + steps) for source in range(first, last)])


def back_dot(grad, weights):
    return lax.dot_general(
        grad, weights, (((1,), (1,)), ((), ())), preferred_element_type=jnp.float32
    )


def outer_dot(act, grad):
    return lax.dot_general(act, grad, (((0,), (0,)), ((), ())), preferred_element_type=jnp.float32)


def plain(resid_in, mlp_out, enc_weight, enc_bias, thresholds, same_dec, next_dec, cross_dec):
    leading = lax.axis_index("sec") == 0
    inputs_full = lax.all_gather(resid_in, "lat", axis=2, tiled=True)
    pre_act = (
        jnp.einsum("ktd,kdc->ktc", inputs_full, enc_weight, preferred_element_type=jnp.float32)
        + enc_bias[:, None, :]
    )
    cut_level = 0.25 * thresholds.astype(jnp.float32)[:, None, :]
    gate_value = jax.nn.sigmoid((pre_act - cut_level) / jump_width)
    latent_act = (pre_act * gate_value).astype(jnp.bfloat16)
    rebuilt_first = jnp.dot(latent_act[0], same_dec[0], preferred_element_type=jnp.float32)
    rebuilt_second = jnp.dot(
        latent_act[1], same_dec[1], preferred_element_type=jnp.float32
    ) + jnp.dot(latent_act[0], next_dec[0], preferred_element_type=jnp.float32)
    far_weight = shifted(cross_dec, "sec", -1)
    source_act = jnp.where(leading, latent_act, jnp.zeros_like(latent_act))
    near_part = jnp.einsum(
        "ktc,kcd->td", source_act, cross_dec[0], preferred_element_type=jnp.float32
    )
    far_part = jnp.einsum(
        "ktc,kcd->td", source_act, far_weight[0], preferred_element_type=jnp.float32
    )
    partials = jnp.stack([rebuilt_first, rebuilt_second, near_part, far_part])
    summed = lax.psum_scatter(partials, "lat", scatter_dimension=2, tiled=True)
    crossing = shifted(summed[2:], "sec", 1)
    rebuilt = summed[:2] + crossing
    misfit = rebuilt - mlp_out.astype(jnp.float32)
    squared_total = lax.psum(jnp.sum(misfit * misfit), ("sec", "lat"))
    mean_square = squared_total / (2.0 * mlp_out.size * lax.axis_size("lat"))
    dy_rows = misfit.astype(jnp.bfloat16)
    extra_rows = shifted(dy_rows, "sec", -1)
    grad_full = lax.all_gather(
        jnp.concatenate([dy_rows, extra_rows], axis=0), "lat", axis=2, tiled=True
    )
    act_grad = jnp.stack(
        [
            back_dot(grad_full[0], same_dec[0]) + back_dot(grad_full[1], next_dec[0]),
            back_dot(grad_full[1], same_dec[1]),
        ]
    )
    cross_grad = jnp.einsum(
        "td,kcd->ktc", grad_full[2], cross_dec[0], preferred_element_type=jnp.float32
    )
    cross_grad = cross_grad + jnp.einsum(
        "td,kcd->ktc", grad_full[3], far_weight[0], preferred_element_type=jnp.float32
    )
    act_grad = act_grad + cross_grad
    gate_slope = gate_value + pre_act * gate_value * (1.0 - gate_value) / jump_width
    pre_grad = act_grad * gate_slope
    grad_bias = jnp.sum(pre_grad, axis=1)
    pre_rounded = pre_grad.astype(jnp.bfloat16)
    grad_enc = jnp.einsum(
        "ktd,ktc->kdc", inputs_full, pre_rounded, preferred_element_type=jnp.float32
    ).astype(jnp.bfloat16)
    grad_same = jnp.stack(
        [outer_dot(latent_act[0], grad_full[0]), outer_dot(latent_act[1], grad_full[1])]
    ).astype(jnp.bfloat16)
    grad_next = outer_dot(latent_act[0], grad_full[1])[None].astype(jnp.bfloat16)
    near_grad = jnp.einsum(
        "ktc,td->kcd", source_act, grad_full[2], preferred_element_type=jnp.float32
    ).astype(jnp.bfloat16)
    far_grad = jnp.einsum(
        "ktc,td->kcd", source_act, grad_full[3], preferred_element_type=jnp.float32
    ).astype(jnp.bfloat16)
    far_back = shifted(far_grad, "sec", 1)
    grad_cross = jnp.where(leading, near_grad, far_back)[None]
    return (mean_square, grad_enc, grad_bias, grad_same, grad_next, grad_cross)


def solution(mesh):
    body = staged if mesh.shape["lat"] == 16 else plain
    in_specs = (
        P("sec", None, "lat"),
        P("sec", None, "lat"),
        P("sec", None, "lat"),
        P("sec", "lat"),
        P("sec", "lat"),
        P("sec", "lat", None),
        P("sec", "lat", None),
        P("sec", None, "lat", None),
    )
    out_specs = (
        P(),
        P("sec", None, "lat"),
        P("sec", "lat"),
        P("sec", "lat", None),
        P("sec", "lat", None),
        P("sec", None, "lat", None),
    )
    return jax.shard_map(body, mesh=mesh, in_specs=in_specs, out_specs=out_specs, check_vma=False)
```

```python
import functools

import jax
import jax.numpy as jnp
from jax import lax
from jax.experimental import pallas as pl
from jax.experimental.pallas import tpu as pltpu
from jax.sharding import PartitionSpec as P

jump_width = 0.1

Z_STEP, Y_STEP, C_STEP = 4, 2, 1

VMEM = pl.BlockSpec(memory_space=pltpu.VMEM)


def dot_nt(a, b):
    return lax.dot_general(a, b, (((1,), (1,)), ((), ())), preferred_element_type=jnp.float32)


def dot_tn(a, b):
    return lax.dot_general(a, b, (((0,), (0,)), ((), ())), preferred_element_type=jnp.float32)


def dot_nn(a, b):
    return lax.dot_general(a, b, (((1,), (0,)), ((), ())), preferred_element_type=jnp.float32)


def place():
    lat = lax.axis_index("lat")
    return lat // Z_STEP, (lat // Y_STEP) % 2, lat % 2


def lanes(start, size):
    return pl.ds(pl.multiple_of(start, 128), size)


def run(kernel, name, outs, *operands, cost=(0, 0)):
    return pl.pallas_call(
        kernel,
        name=name,
        out_shape=[jax.ShapeDtypeStruct(shape, dtype) for shape, dtype in outs],
        in_specs=[VMEM] * len(operands),
        out_specs=[VMEM] * len(outs),
        compiler_params=pltpu.CompilerParams(vmem_limit_bytes=48 * 1024 * 1024),
        cost_estimate=pl.CostEstimate(flops=cost[0], bytes_accessed=cost[1], transcendentals=0),
    )(*operands)


def to_lat(value, step):
    return lax.ppermute(value, "lat", [(source, source ^ step) for source in range(lax.axis_size("lat"))])


def to_both(value, sec_pairs, step):
    count = lax.axis_size("lat")
    pairs = [(a * count + lat, b * count + (lat ^ step)) for a, b in sec_pairs for lat in range(count)]
    return lax.ppermute(value, ("sec", "lat"), pairs)


SWAP = [(0, 1), (1, 0)]


def pack_kernel(same, nxt, cross, own_s, own_x, far_s, far_x, same_v, nxt_v, cross_v, sems):
    _, y, _ = place()
    width = own_s.shape[-1] // 4
    copies = [
        pltpu.make_async_copy(source, target, sems.at[n])
        for n, (source, target) in enumerate(((cross.at[0], cross_v), (same, same_v), (nxt.at[0], nxt_v)))
    ]
    for copy in copies:
        copy.start()

    def move(source, plain, row, crossed):
        for z in range(4):
            to = slice(z * width, (z + 1) * width)
            for half, out in enumerate((plain, crossed)):
                out[row, :, to] = source[:, lanes(z * 2 * width + (y + half) % 2 * width, width)]

    copies[0].wait()
    for j in range(2):
        move(cross_v.at[j], own_x, j, far_x)
    copies[1].wait()
    for layer in range(2):
        move(same_v.at[layer], own_s, layer, far_s)
    copies[2].wait()
    move(nxt_v, own_s, 2, far_s)


def stacked(ref, first, last):
    return ref[first:last].reshape((last - first) * ref.shape[1], ref.shape[2])


def pair_kernel(own, other, pair):
    pair[0] = own[...]
    pair[1] = other[...]


def relay_kernel(line1, line3, lines):
    lines[0] = line1[...]
    lines[1] = line3[...]


def row_kernel(one, two, row):
    row[0] = one[...]
    row[1] = two[...]


def last_kernel(own, line1, line2, line3, row, lead):
    row[0] = line2[...]
    row[1] = line3[...]
    for k, part in enumerate((own, line1, line2, line3)):
        lead[k] = part[0]


def encode_kernel(*refs):
    pieces, (weight, bias, cut, full, slope, act) = refs[:8], refs[8:]
    z, y, c = place()
    block = pieces[0].shape[-1]

    def put(k, j, core, layer, value):
        home = (z ^ k) * Z_STEP + (y ^ j) * Y_STEP + (c ^ core)
        full[layer, :, lanes(home * block, block)] = value

    for core in range(2):
        mine, lines, line2, line2_y = pieces[core * 4 : core * 4 + 4]
        for layer in range(2):
            for j in range(2):
                put(0, j, core, layer, mine[j, layer])
                put(1, j, core, layer, lines[0, j, layer])
                put(3, j, core, layer, lines[1, j, layer])
            put(2, 0, core, layer, line2[layer])
            put(2, 1, core, layer, line2_y[layer])
    for layer in range(2):
        pre = dot_nt(weight[layer], full[layer]) + bias[layer]
        gate = jax.nn.sigmoid((pre - cut[layer]) / jump_width)
        act[layer] = (pre * gate).astype(jnp.bfloat16)
        slope[layer] = gate + pre * gate * (1.0 - gate) / jump_width


def decode_kernel(act, act_y, act_x, act_d, own_s, own_x, peer_s, peer_x, near_x, diag_x, send, keep):
    _, _, c = place()
    leading = lax.axis_index("sec") == 0
    across, diagonal = (
        jnp.where(leading, jnp.zeros((128, 128), jnp.bfloat16), stacked(ref, 0, 2)) for ref in (act_x, act_d)
    )
    first = dot_tn(jnp.concatenate([act[0], act_y[0]]), jnp.concatenate([own_s[0], peer_s[0]]))
    first += dot_tn(across, stacked(near_x, 0, 2))
    first += dot_tn(diagonal, stacked(diag_x, 0, 2))
    second = dot_tn(jnp.concatenate([act[1], act[0]]), stacked(own_s, 1, 3))
    second += dot_tn(jnp.concatenate([act_y[1], act_y[0]]), stacked(peer_s, 1, 3))
    second += dot_tn(across, stacked(own_x, 0, 2))
    second += dot_tn(diagonal, stacked(peer_x, 0, 2))
    block = send.shape[-1]
    for layer, total in enumerate((first, second)):
        for z in range(4):
            low = total[:, z * 2 * block : z * 2 * block + block]
            high = total[:, z * 2 * block + block : (z + 1) * 2 * block]
            keep[z, layer] = jnp.where(c == 0, low, high)
            send[z, layer] = jnp.where(c == 0, high, low).astype(jnp.bfloat16)


def fold_kernel(keep, got, mine, s1, s2, s3):
    z, _, _ = place()
    mine[...] = keep[z] + got[z].astype(jnp.float32)
    for k, out in ((1, s1), (2, s2), (3, s3)):
        out[...] = (keep[z ^ k] + got[z ^ k].astype(jnp.float32)).astype(jnp.bfloat16)


def misfit_kernel(mine, g1, g2, g3, target, dy):
    total = mine[...] + g1[...].astype(jnp.float32) + g2[...].astype(jnp.float32) + g3[...].astype(jnp.float32)
    dy[...] = (total - target[...].astype(jnp.float32)).astype(jnp.bfloat16)


def act_grad_kernel(near, near_core, last, last_core, own_s, own_x, peer_s, peer_x, near_x, diag_x, half, grad_own, to_y, to_x, to_d):
    z, _, c = place()
    block = near.shape[-1]
    for k in range(4):
        mine, core = ((near, near_core), (last, last_core))[k // 2]
        for layer in range(2):
            half[layer, :, lanes(((z ^ k) * 2 + c) * block, block)] = mine[k % 2, layer]
            half[layer, :, lanes(((z ^ k) * 2 + 1 - c) * block, block)] = core[k % 2, layer]
    first, second = half[0], half[1]
    a = dot_nt(stacked(own_s, 1, 3), second)
    grad_own[0] = a[64:128] + dot_nt(own_s[0], first)
    grad_own[1] = a[0:64]
    a = dot_nt(stacked(peer_s, 1, 3), second)
    to_y[0:64] = (a[64:128] + dot_nt(peer_s[0], first)).astype(jnp.bfloat16)
    to_y[64:128] = a[0:64].astype(jnp.bfloat16)
    to_x[0:128] = (dot_nt(stacked(own_x, 0, 2), second) + dot_nt(stacked(near_x, 0, 2), first)).astype(jnp.bfloat16)
    to_d[0:128] = (dot_nt(stacked(peer_x, 0, 2), second) + dot_nt(stacked(diag_x, 0, 2), first)).astype(jnp.bfloat16)
    wide = half[...].astype(jnp.float32)
    squares = jnp.sum((wide * wide).reshape(-1, 8, wide.shape[-1]), axis=0)
    part = sum(squares[:, n * 128 : n * 128 + 128] for n in range(squares.shape[1] // 128))
    high = part.astype(jnp.bfloat16)
    low = (part - high.astype(jnp.float32)).astype(jnp.bfloat16)
    for out in (to_y, to_x, to_d):
        out[128:144] = jnp.concatenate([high, low])
    grad_own[2, 0:8] = part


def encoder_grad_kernel(entries, grad_own, from_y, from_x, from_d, slope, full, mean_square, grad_enc, grad_bias):
    leading = lax.axis_index("sec") == 0
    wide = [ref[...].astype(jnp.float32) for ref in (from_y, from_x, from_d)]
    squares = grad_own[2, 0:8] + sum(part[128:136] + part[136:144] for part in wide)
    mean_square[...] = jnp.sum(squares, keepdims=True) / entries
    for layer in range(2):
        rows = slice(layer * 64, layer * 64 + 64)
        across = wide[1][rows] + wide[2][rows]
        total = grad_own[layer] + wide[0][rows] + jnp.where(leading, across, jnp.zeros_like(across))
        pre_grad = total * slope[layer]
        grad_bias[layer : layer + 1] = jnp.sum(pre_grad.T, axis=0, keepdims=True)
        grad_enc[layer] = dot_nn(pre_grad.astype(jnp.bfloat16), full[layer]).astype(jnp.bfloat16)


def decoder_grad_kernel(act, act_x, half, far, last, far_core, last_core, x_own, x_core, d_own, d_core, grad_same, grad_next, grad_cross, dy, dx):
    z, y, c = place()
    leading = lax.axis_index("sec") == 0
    block = far.shape[-1]
    for layer in range(2):
        for n in range(4):
            dy[layer, :, lanes((n * 2 + y) * 2 * block, 2 * block)] = half[layer, :, n * 2 * block : (n + 1) * 2 * block]
        for k in range(4):
            home = (z ^ k) * Z_STEP + (1 - y) * Y_STEP
            mine, core = ((far, far_core), (last, last_core))[k // 2]
            dy[layer, :, lanes((home + c) * block, block)] = mine[k % 2, layer]
            dy[layer, :, lanes((home + 1 - c) * block, block)] = core[k % 2, layer]
    both = jnp.concatenate([act[0], act[1]])
    grad_same[0] = dot_nn(act[0], dy[0]).astype(jnp.bfloat16)
    second = dot_nn(both, dy[1]).astype(jnp.bfloat16)
    grad_next[0] = second[0:64]
    grad_same[1] = second[64:128]

    @pl.when(leading)
    def _():
        for k in range(4):
            for row, own, core in ((y, x_own, x_core), (1 - y, d_own, d_core)):
                home = (z ^ k) * Z_STEP + row * Y_STEP
                dx[:, lanes((home + c) * block, block)] = own[k]
                dx[:, lanes((home + 1 - c) * block, block)] = core[k]
        grad_cross[0] = dot_nn(both, dx[...]).astype(jnp.bfloat16).reshape(2, 64, -1)

    @pl.when(jnp.logical_not(leading))
    def _():
        grad_cross[0] = dot_nn(act_x[...].reshape(128, 128), dy[1]).astype(jnp.bfloat16).reshape(2, 64, -1)


def staged(resid_in, mlp_out, enc_weight, enc_bias, thresholds, same_dec, next_dec, cross_dec):
    bf16, f32 = jnp.bfloat16, jnp.float32
    depth = same_dec.shape[-1]
    block = resid_in.shape[-1]
    entries = 2.0 * resid_in.size * lax.axis_size("lat")
    tall = jnp.swapaxes(enc_weight, 1, 2)
    bias = jnp.broadcast_to(enc_bias[:, :, None], (2, 64, 128))
    cut = jnp.broadcast_to(0.25 * thresholds.astype(f32)[:, :, None], (2, 64, 128))

    other = to_lat(resid_in, Y_STEP)
    line2 = to_lat(resid_in, 2 * Z_STEP)
    shapes = [((3, 64, depth // 2), bf16), ((2, 64, depth // 2), bf16)] * 2
    own_s, own_x, far_s, far_x = pl.pallas_call(
        pack_kernel,
        name="pack",
        out_shape=[jax.ShapeDtypeStruct(shape, dtype) for shape, dtype in shapes],
        in_specs=[pl.BlockSpec(memory_space=pl.ANY)] * 3,
        out_specs=[VMEM] * 4,
        scratch_shapes=[
            pltpu.VMEM((2, 64, depth), bf16),
            pltpu.VMEM((64, depth), bf16),
            pltpu.VMEM((2, 64, depth), bf16),
            pltpu.SemaphoreType.DMA((3,)),
        ],
    )(same_dec, next_dec, cross_dec)
    (near,) = run(pair_kernel, "pair", [((2, 2, 128, block), bf16)], resid_in, other)
    line1, line3 = (to_lat(near, k * Z_STEP) for k in (1, 3))
    line2, far_x, _ = lax.optimization_barrier((line2, far_x, near))
    line2_y = to_lat(line2, Y_STEP)
    peer_x = to_lat(far_x, Y_STEP)
    lead_x, _ = lax.optimization_barrier((own_x, other))
    near_x = to_both(lead_x, SWAP, 0)
    far_s, line2_y = lax.optimization_barrier((far_s, line2_y))
    peer_s = to_lat(far_s, Y_STEP)
    diag_x = to_both(peer_x, SWAP, 0)
    (lines,) = run(relay_kernel, "relay", [((2, 2, 2, 128, block), bf16)], line1, line3, cost=(1_000_000_000, 0))
    lines, near_x = lax.optimization_barrier((lines, near_x))
    pieces = [near, lines, line2, line2_y]
    pieces += [to_lat(piece, C_STEP) for piece in pieces]
    full, slope, act = run(
        encode_kernel, "encode",
        [((2, 128, depth), bf16), ((2, 64, 128), f32), ((2, 64, 128), bf16)],
        *pieces, tall, bias, cut,
    )
    act_y = to_lat(act, Y_STEP)
    act_x = to_both(act, SWAP, 0)
    act_d = to_both(act, SWAP, Y_STEP)
    send, keep = run(
        decode_kernel, "decode",
        [((4, 2, 128, block), bf16), ((4, 2, 128, block), f32)],
        act, act_y, act_x, act_d, own_s, own_x, peer_s, peer_x, near_x, diag_x,
    )
    got = to_lat(send, C_STEP)
    mine, *parts = run(
        fold_kernel, "fold",
        [((2, 128, block), f32)] + [((2, 128, block), bf16)] * 3,
        keep, got,
    )
    parts = [to_lat(part, k * Z_STEP) for k, part in zip((1, 2, 3), parts)]
    (dy,) = run(misfit_kernel, "misfit", [((2, 128, block), bf16)], mine, *parts, mlp_out)
    pair = ((2, 2, 128, block), bf16)
    line1, line2, line3 = (to_lat(dy, k * Z_STEP) for k in (1, 2, 3))
    (row,) = run(row_kernel, "row", [pair], dy, line1)
    far = to_lat(row, Y_STEP)
    row_core = to_lat(row, C_STEP)
    last, lead = run(last_kernel, "last", [pair, ((4, 128, block), bf16)], dy, line1, line2, line3, cost=(2_000_000_000, 0))
    last, lead, far = lax.optimization_barrier((last, lead, far))
    far_core = to_lat(far, C_STEP)
    last_core = to_lat(last, C_STEP)
    far_last = to_lat(last, Y_STEP)
    x_own = to_both(lead, SWAP, 0)
    d_own = to_both(lead, SWAP, Y_STEP)
    half, grad_own, to_y, to_x, to_d = run(
        act_grad_kernel, "act_grad",
        [((2, 128, depth // 2), bf16), ((3, 64, 128), f32)] + [((144, 128), bf16)] * 3,
        row, row_core, last, last_core, own_s, own_x, peer_s, peer_x, near_x, diag_x,
    )
    from_y = to_lat(to_y, Y_STEP)
    from_x = to_both(to_x, SWAP, 0)
    from_d = to_both(to_d, SWAP, Y_STEP)
    mean_square, grad_enc, grad_bias = run(
        functools.partial(encoder_grad_kernel, entries), "encoder_grad",
        [((1, 1), f32), ((2, 64, depth), bf16), ((2, 64), f32)],
        grad_own, from_y, from_x, from_d, slope, full,
    )
    far_last, x_own, d_own, _ = lax.optimization_barrier((far_last, x_own, d_own, (from_y, from_x, from_d)))
    last_far_core = to_lat(far_last, C_STEP)
    x_core = to_lat(x_own, C_STEP)
    d_core = to_lat(d_own, C_STEP)
    operands = (act, act_x, half, far, far_last, far_core, last_far_core, x_own, x_core, d_own, d_core)
    outs = [((2, 64, depth), bf16), ((1, 64, depth), bf16), ((1, 2, 64, depth), bf16)]
    grad_same, grad_next, grad_cross = pl.pallas_call(
        decoder_grad_kernel,
        name="decoder_grad",
        out_shape=[jax.ShapeDtypeStruct(shape, dtype) for shape, dtype in outs],
        in_specs=[VMEM] * len(operands),
        out_specs=[VMEM] * len(outs),
        scratch_shapes=[pltpu.VMEM((2, 128, depth), bf16), pltpu.VMEM((128, depth), bf16)],
        compiler_params=pltpu.CompilerParams(vmem_limit_bytes=48 * 1024 * 1024),
    )(*operands)
    return (mean_square[0, 0], jnp.swapaxes(grad_enc, 1, 2), grad_bias, grad_same, grad_next, grad_cross)


def shifted(value, axis, steps):
    count = lax.axis_size(axis)
    first, last = (max(0, -steps), min(count, count - steps))
    return lax.ppermute(value, axis, [(source, source + steps) for source in range(first, last)])


def back_dot(grad, weights):
    return lax.dot_general(
        grad, weights, (((1,), (1,)), ((), ())), preferred_element_type=jnp.float32
    )


def outer_dot(act, grad):
    return lax.dot_general(act, grad, (((0,), (0,)), ((), ())), preferred_element_type=jnp.float32)


def plain(resid_in, mlp_out, enc_weight, enc_bias, thresholds, same_dec, next_dec, cross_dec):
    leading = lax.axis_index("sec") == 0
    inputs_full = lax.all_gather(resid_in, "lat", axis=2, tiled=True)
    pre_act = (
        jnp.einsum("ktd,kdc->ktc", inputs_full, enc_weight, preferred_element_type=jnp.float32)
        + enc_bias[:, None, :]
    )
    cut_level = 0.25 * thresholds.astype(jnp.float32)[:, None, :]
    gate_value = jax.nn.sigmoid((pre_act - cut_level) / jump_width)
    latent_act = (pre_act * gate_value).astype(jnp.bfloat16)
    rebuilt_first = jnp.dot(latent_act[0], same_dec[0], preferred_element_type=jnp.float32)
    rebuilt_second = jnp.dot(
        latent_act[1], same_dec[1], preferred_element_type=jnp.float32
    ) + jnp.dot(latent_act[0], next_dec[0], preferred_element_type=jnp.float32)
    far_weight = shifted(cross_dec, "sec", -1)
    source_act = jnp.where(leading, latent_act, jnp.zeros_like(latent_act))
    near_part = jnp.einsum(
        "ktc,kcd->td", source_act, cross_dec[0], preferred_element_type=jnp.float32
    )
    far_part = jnp.einsum(
        "ktc,kcd->td", source_act, far_weight[0], preferred_element_type=jnp.float32
    )
    partials = jnp.stack([rebuilt_first, rebuilt_second, near_part, far_part])
    summed = lax.psum_scatter(partials, "lat", scatter_dimension=2, tiled=True)
    crossing = shifted(summed[2:], "sec", 1)
    rebuilt = summed[:2] + crossing
    misfit = rebuilt - mlp_out.astype(jnp.float32)
    squared_total = lax.psum(jnp.sum(misfit * misfit), ("sec", "lat"))
    mean_square = squared_total / (2.0 * mlp_out.size * lax.axis_size("lat"))
    dy_rows = misfit.astype(jnp.bfloat16)
    extra_rows = shifted(dy_rows, "sec", -1)
    grad_full = lax.all_gather(
        jnp.concatenate([dy_rows, extra_rows], axis=0), "lat", axis=2, tiled=True
    )
    act_grad = jnp.stack(
        [
            back_dot(grad_full[0], same_dec[0]) + back_dot(grad_full[1], next_dec[0]),
            back_dot(grad_full[1], same_dec[1]),
        ]
    )
    cross_grad = jnp.einsum(
        "td,kcd->ktc", grad_full[2], cross_dec[0], preferred_element_type=jnp.float32
    )
    cross_grad = cross_grad + jnp.einsum(
        "td,kcd->ktc", grad_full[3], far_weight[0], preferred_element_type=jnp.float32
    )
    act_grad = act_grad + cross_grad
    gate_slope = gate_value + pre_act * gate_value * (1.0 - gate_value) / jump_width
    pre_grad = act_grad * gate_slope
    grad_bias = jnp.sum(pre_grad, axis=1)
    pre_rounded = pre_grad.astype(jnp.bfloat16)
    grad_enc = jnp.einsum(
        "ktd,ktc->kdc", inputs_full, pre_rounded, preferred_element_type=jnp.float32
    ).astype(jnp.bfloat16)
    grad_same = jnp.stack(
        [outer_dot(latent_act[0], grad_full[0]), outer_dot(latent_act[1], grad_full[1])]
    ).astype(jnp.bfloat16)
    grad_next = outer_dot(latent_act[0], grad_full[1])[None].astype(jnp.bfloat16)
    near_grad = jnp.einsum(
        "ktc,td->kcd", source_act, grad_full[2], preferred_element_type=jnp.float32
    ).astype(jnp.bfloat16)
    far_grad = jnp.einsum(
        "ktc,td->kcd", source_act, grad_full[3], preferred_element_type=jnp.float32
    ).astype(jnp.bfloat16)
    far_back = shifted(far_grad, "sec", 1)
    grad_cross = jnp.where(leading, near_grad, far_back)[None]
    return (mean_square, grad_enc, grad_bias, grad_same, grad_next, grad_cross)


def solution(mesh):
    body = staged if mesh.shape["lat"] == 16 else plain
    in_specs = (
        P("sec", None, "lat"),
        P("sec", None, "lat"),
        P("sec", None, "lat"),
        P("sec", "lat"),
        P("sec", "lat"),
        P("sec", "lat", None),
        P("sec", "lat", None),
        P("sec", None, "lat", None),
    )
    out_specs = (
        P(),
        P("sec", None, "lat"),
        P("sec", "lat"),
        P("sec", "lat", None),
        P("sec", "lat", None),
        P("sec", None, "lat", None),
    )
    return jax.shard_map(body, mesh=mesh, in_specs=in_specs, out_specs=out_specs, check_vma=False)
```

```python
import functools

import jax
import jax.numpy as jnp
from jax import lax
from jax.experimental import pallas as pl
from jax.experimental.pallas import tpu as pltpu
from jax.sharding import PartitionSpec as P

jump_width = 0.1

Z_STEP, Y_STEP, C_STEP = 4, 2, 1

VMEM = pl.BlockSpec(memory_space=pltpu.VMEM)


def dot_nt(a, b):
    return lax.dot_general(a, b, (((1,), (1,)), ((), ())), preferred_element_type=jnp.float32)


def dot_tn(a, b):
    return lax.dot_general(a, b, (((0,), (0,)), ((), ())), preferred_element_type=jnp.float32)


def dot_nn(a, b):
    return lax.dot_general(a, b, (((1,), (0,)), ((), ())), preferred_element_type=jnp.float32)


def place():
    lat = lax.axis_index("lat")
    return lat // Z_STEP, (lat // Y_STEP) % 2, lat % 2


def lanes(start, size):
    return pl.ds(pl.multiple_of(start, 128), size)


def run(kernel, name, outs, *operands, cost=(0, 0)):
    return pl.pallas_call(
        kernel,
        name=name,
        out_shape=[jax.ShapeDtypeStruct(shape, dtype) for shape, dtype in outs],
        in_specs=[VMEM] * len(operands),
        out_specs=[VMEM] * len(outs),
        compiler_params=pltpu.CompilerParams(vmem_limit_bytes=48 * 1024 * 1024),
        cost_estimate=pl.CostEstimate(flops=cost[0], bytes_accessed=cost[1], transcendentals=0),
    )(*operands)


def to_lat(value, step):
    return lax.ppermute(value, "lat", [(source, source ^ step) for source in range(lax.axis_size("lat"))])


def to_both(value, sec_pairs, step):
    count = lax.axis_size("lat")
    pairs = [(a * count + lat, b * count + (lat ^ step)) for a, b in sec_pairs for lat in range(count)]
    return lax.ppermute(value, ("sec", "lat"), pairs)


SWAP = [(0, 1), (1, 0)]


def pack_kernel(same, nxt, cross, own_s, own_x, far_s, far_x, same_v, nxt_v, cross_v, sems):
    _, y, _ = place()
    width = own_s.shape[-1] // 4
    copies = [
        pltpu.make_async_copy(source, target, sems.at[n])
        for n, (source, target) in enumerate(((cross.at[0], cross_v), (same, same_v), (nxt.at[0], nxt_v)))
    ]
    for copy in copies:
        copy.start()

    def move(source, plain, row, crossed):
        for z in range(4):
            to = slice(z * width, (z + 1) * width)
            for half, out in enumerate((plain, crossed)):
                out[row, :, to] = source[:, lanes(z * 2 * width + (y + half) % 2 * width, width)]

    copies[0].wait()
    for j in range(2):
        move(cross_v.at[j], own_x, j, far_x)
    copies[1].wait()
    for layer in range(2):
        move(same_v.at[layer], own_s, layer, far_s)
    copies[2].wait()
    move(nxt_v, own_s, 2, far_s)


def stacked(ref, first, last):
    return ref[first:last].reshape((last - first) * ref.shape[1], ref.shape[2])


def pair_kernel(own, other, pair):
    pair[0] = own[...]
    pair[1] = other[...]


def relay_kernel(line1, line3, lines):
    lines[0] = line1[...]
    lines[1] = line3[...]


def row_kernel(one, two, row):
    row[0] = one[...]
    row[1] = two[...]


def last_kernel(own, line1, line2, line3, row, lead):
    row[0] = line2[...]
    row[1] = line3[...]
    for k, part in enumerate((own, line1, line2, line3)):
        lead[k] = part[0]


def encode_kernel(*refs):
    pieces, (weight, bias, cut, full, slope, act) = refs[:8], refs[8:]
    z, y, c = place()
    block = pieces[0].shape[-1]

    def put(k, j, core, layer, value):
        home = (z ^ k) * Z_STEP + (y ^ j) * Y_STEP + (c ^ core)
        full[layer, :, lanes(home * block, block)] = value

    for core in range(2):
        mine, lines, line2, line2_y = pieces[core * 4 : core * 4 + 4]
        for layer in range(2):
            for j in range(2):
                put(0, j, core, layer, mine[j, layer])
                put(1, j, core, layer, lines[0, j, layer])
                put(3, j, core, layer, lines[1, j, layer])
            put(2, 0, core, layer, line2[layer])
            put(2, 1, core, layer, line2_y[layer])
    for layer in range(2):
        pre = dot_nt(weight[layer], full[layer]) + bias[layer]
        gate = jax.nn.sigmoid((pre - cut[layer]) / jump_width)
        act[layer] = (pre * gate).astype(jnp.bfloat16)
        slope[layer] = gate + pre * gate * (1.0 - gate) / jump_width


def decode_kernel(act, act_y, act_x, act_d, own_s, own_x, peer_s, peer_x, near_x, diag_x, send, keep):
    _, _, c = place()
    leading = lax.axis_index("sec") == 0
    across, diagonal = (
        jnp.where(leading, jnp.zeros((128, 128), jnp.bfloat16), stacked(ref, 0, 2)) for ref in (act_x, act_d)
    )
    first = dot_tn(jnp.concatenate([act[0], act_y[0]]), jnp.concatenate([own_s[0], peer_s[0]]))
    first += dot_tn(across, stacked(near_x, 0, 2))
    first += dot_tn(diagonal, stacked(diag_x, 0, 2))
    second = dot_tn(jnp.concatenate([act[1], act[0]]), stacked(own_s, 1, 3))
    second += dot_tn(jnp.concatenate([act_y[1], act_y[0]]), stacked(peer_s, 1, 3))
    second += dot_tn(across, stacked(own_x, 0, 2))
    second += dot_tn(diagonal, stacked(peer_x, 0, 2))
    block = send.shape[-1]
    for layer, total in enumerate((first, second)):
        for z in range(4):
            low = total[:, z * 2 * block : z * 2 * block + block]
            high = total[:, z * 2 * block + block : (z + 1) * 2 * block]
            keep[z, layer] = jnp.where(c == 0, low, high)
            send[z, layer] = jnp.where(c == 0, high, low).astype(jnp.bfloat16)


def fold_kernel(keep, got, mine, s1, s2, s3):
    z, _, _ = place()
    mine[...] = keep[z] + got[z].astype(jnp.float32)
    for k, out in ((1, s1), (2, s2), (3, s3)):
        out[...] = (keep[z ^ k] + got[z ^ k].astype(jnp.float32)).astype(jnp.bfloat16)


def misfit_kernel(mine, g1, g2, g3, target, dy):
    total = mine[...] + g1[...].astype(jnp.float32) + g2[...].astype(jnp.float32) + g3[...].astype(jnp.float32)
    dy[...] = (total - target[...].astype(jnp.float32)).astype(jnp.bfloat16)


def act_grad_kernel(near, near_core, last, last_core, own_s, own_x, peer_s, peer_x, near_x, diag_x, half, grad_own, to_y, to_x, to_d):
    z, _, c = place()
    block = near.shape[-1]
    for k in range(4):
        mine, core = ((near, near_core), (last, last_core))[k // 2]
        for layer in range(2):
            half[layer, :, lanes(((z ^ k) * 2 + c) * block, block)] = mine[k % 2, layer]
            half[layer, :, lanes(((z ^ k) * 2 + 1 - c) * block, block)] = core[k % 2, layer]
    first, second = half[0], half[1]
    a = dot_nt(stacked(own_s, 1, 3), second)
    grad_own[0] = a[64:128] + dot_nt(own_s[0], first)
    grad_own[1] = a[0:64]
    a = dot_nt(stacked(peer_s, 1, 3), second)
    to_y[0:64] = (a[64:128] + dot_nt(peer_s[0], first)).astype(jnp.bfloat16)
    to_y[64:128] = a[0:64].astype(jnp.bfloat16)
    to_x[0:128] = (dot_nt(stacked(own_x, 0, 2), second) + dot_nt(stacked(near_x, 0, 2), first)).astype(jnp.bfloat16)
    to_d[0:128] = (dot_nt(stacked(peer_x, 0, 2), second) + dot_nt(stacked(diag_x, 0, 2), first)).astype(jnp.bfloat16)
    wide = half[...].astype(jnp.float32)
    squares = jnp.sum((wide * wide).reshape(-1, 8, wide.shape[-1]), axis=0)
    part = sum(squares[:, n * 128 : n * 128 + 128] for n in range(squares.shape[1] // 128))
    high = part.astype(jnp.bfloat16)
    low = (part - high.astype(jnp.float32)).astype(jnp.bfloat16)
    for out in (to_y, to_x, to_d):
        out[128:144] = jnp.concatenate([high, low])
    grad_own[2, 0:8] = part


def encoder_grad_kernel(entries, grad_own, from_y, from_x, from_d, slope, full, mean_square, grad_enc, grad_bias):
    leading = lax.axis_index("sec") == 0
    wide = [ref[...].astype(jnp.float32) for ref in (from_y, from_x, from_d)]
    squares = grad_own[2, 0:8] + sum(part[128:136] + part[136:144] for part in wide)
    mean_square[...] = jnp.sum(squares, keepdims=True) / entries
    for layer in range(2):
        rows = slice(layer * 64, layer * 64 + 64)
        across = wide[1][rows] + wide[2][rows]
        total = grad_own[layer] + wide[0][rows] + jnp.where(leading, across, jnp.zeros_like(across))
        pre_grad = total * slope[layer]
        grad_bias[layer : layer + 1] = jnp.sum(pre_grad.T, axis=0, keepdims=True)
        grad_enc[layer] = dot_nn(pre_grad.astype(jnp.bfloat16), full[layer]).astype(jnp.bfloat16)


def decoder_grad_kernel(act, act_x, half, far, last, far_core, last_core, x_own, x_core, d_own, d_core, grad_same, grad_next, grad_cross, dy, dx, staged_out, sems):
    z, y, c = place()
    leading = lax.axis_index("sec") == 0
    block = far.shape[-1]
    for layer in range(2):
        for n in range(4):
            dy[layer, :, lanes((n * 2 + y) * 2 * block, 2 * block)] = half[layer, :, n * 2 * block : (n + 1) * 2 * block]
        for k in range(4):
            home = (z ^ k) * Z_STEP + (1 - y) * Y_STEP
            mine, core = ((far, far_core), (last, last_core))[k // 2]
            dy[layer, :, lanes((home + c) * block, block)] = mine[k % 2, layer]
            dy[layer, :, lanes((home + 1 - c) * block, block)] = core[k % 2, layer]
    copies = []

    def out(value, stage, target):
        stage[...] = value.astype(jnp.bfloat16)
        copies.append(pltpu.make_async_copy(stage, target, sems.at[len(copies)]))
        copies[-1].start()

    both = jnp.concatenate([act[0], act[1]])
    second = dot_nn(both, dy[1])
    out(second[0:64], staged_out.at[0], grad_next.at[0])
    out(second[64:128], staged_out.at[1], grad_same.at[1])
    out(dot_nn(act[0], dy[0]), staged_out.at[2], grad_same.at[0])

    @pl.when(leading)
    def _():
        for k in range(4):
            for row, own, core in ((y, x_own, x_core), (1 - y, d_own, d_core)):
                home = (z ^ k) * Z_STEP + row * Y_STEP
                dx[:, lanes((home + c) * block, block)] = own[k]
                dx[:, lanes((home + 1 - c) * block, block)] = core[k]

    @pl.when(jnp.logical_not(leading))
    def _():
        dx[...] = dy[1]

    source = jnp.where(leading, both, stacked(act_x, 0, 2))
    for j in range(2):
        out(dot_nn(source[j * 64 : j * 64 + 64], dx[...]), staged_out.at[3 + j], grad_cross.at[0, j])
    for copy in copies:
        copy.wait()


def staged(resid_in, mlp_out, enc_weight, enc_bias, thresholds, same_dec, next_dec, cross_dec):
    bf16, f32 = jnp.bfloat16, jnp.float32
    depth = same_dec.shape[-1]
    block = resid_in.shape[-1]
    entries = 2.0 * resid_in.size * lax.axis_size("lat")
    tall = jnp.swapaxes(enc_weight, 1, 2)
    bias = jnp.broadcast_to(enc_bias[:, :, None], (2, 64, 128))
    cut = jnp.broadcast_to(0.25 * thresholds.astype(f32)[:, :, None], (2, 64, 128))

    other = to_lat(resid_in, Y_STEP)
    line2 = to_lat(resid_in, 2 * Z_STEP)
    shapes = [((3, 64, depth // 2), bf16), ((2, 64, depth // 2), bf16)] * 2
    own_s, own_x, far_s, far_x = pl.pallas_call(
        pack_kernel,
        name="pack",
        out_shape=[jax.ShapeDtypeStruct(shape, dtype) for shape, dtype in shapes],
        in_specs=[pl.BlockSpec(memory_space=pl.ANY)] * 3,
        out_specs=[VMEM] * 4,
        scratch_shapes=[
            pltpu.VMEM((2, 64, depth), bf16),
            pltpu.VMEM((64, depth), bf16),
            pltpu.VMEM((2, 64, depth), bf16),
            pltpu.SemaphoreType.DMA((3,)),
        ],
    )(same_dec, next_dec, cross_dec)
    (near,) = run(pair_kernel, "pair", [((2, 2, 128, block), bf16)], resid_in, other)
    line1, line3 = (to_lat(near, k * Z_STEP) for k in (1, 3))
    line2, far_x, _ = lax.optimization_barrier((line2, far_x, near))
    line2_y = to_lat(line2, Y_STEP)
    peer_x = to_lat(far_x, Y_STEP)
    lead_x, _ = lax.optimization_barrier((own_x, other))
    near_x = to_both(lead_x, SWAP, 0)
    far_s, line2_y = lax.optimization_barrier((far_s, line2_y))
    peer_s = to_lat(far_s, Y_STEP)
    diag_x = to_both(peer_x, SWAP, 0)
    (lines,) = run(relay_kernel, "relay", [((2, 2, 2, 128, block), bf16)], line1, line3, cost=(1_000_000_000, 0))
    lines, near_x = lax.optimization_barrier((lines, near_x))
    pieces = [near, lines, line2, line2_y]
    pieces += [to_lat(piece, C_STEP) for piece in pieces]
    full, slope, act = run(
        encode_kernel, "encode",
        [((2, 128, depth), bf16), ((2, 64, 128), f32), ((2, 64, 128), bf16)],
        *pieces, tall, bias, cut,
    )
    act_y = to_lat(act, Y_STEP)
    act_x = to_both(act, SWAP, 0)
    act_d = to_both(act, SWAP, Y_STEP)
    send, keep = run(
        decode_kernel, "decode",
        [((4, 2, 128, block), bf16), ((4, 2, 128, block), f32)],
        act, act_y, act_x, act_d, own_s, own_x, peer_s, peer_x, near_x, diag_x,
    )
    got = to_lat(send, C_STEP)
    mine, *parts = run(
        fold_kernel, "fold",
        [((2, 128, block), f32)] + [((2, 128, block), bf16)] * 3,
        keep, got,
    )
    parts = [to_lat(part, k * Z_STEP) for k, part in zip((1, 2, 3), parts)]
    (dy,) = run(misfit_kernel, "misfit", [((2, 128, block), bf16)], mine, *parts, mlp_out)
    pair = ((2, 2, 128, block), bf16)
    line1, line2, line3 = (to_lat(dy, k * Z_STEP) for k in (1, 2, 3))
    (row,) = run(row_kernel, "row", [pair], dy, line1)
    far = to_lat(row, Y_STEP)
    row_core = to_lat(row, C_STEP)
    last, lead = run(last_kernel, "last", [pair, ((4, 128, block), bf16)], dy, line1, line2, line3, cost=(2_000_000_000, 0))
    last, lead, far = lax.optimization_barrier((last, lead, far))
    far_core = to_lat(far, C_STEP)
    last_core = to_lat(last, C_STEP)
    far_last = to_lat(last, Y_STEP)
    x_own = to_both(lead, SWAP, 0)
    d_own = to_both(lead, SWAP, Y_STEP)
    half, grad_own, to_y, to_x, to_d = run(
        act_grad_kernel, "act_grad",
        [((2, 128, depth // 2), bf16), ((3, 64, 128), f32)] + [((144, 128), bf16)] * 3,
        row, row_core, last, last_core, own_s, own_x, peer_s, peer_x, near_x, diag_x,
    )
    from_y = to_lat(to_y, Y_STEP)
    from_x = to_both(to_x, SWAP, 0)
    from_d = to_both(to_d, SWAP, Y_STEP)
    mean_square, grad_enc, grad_bias = run(
        functools.partial(encoder_grad_kernel, entries), "encoder_grad",
        [((1, 1), f32), ((2, 64, depth), bf16), ((2, 64), f32)],
        grad_own, from_y, from_x, from_d, slope, full,
    )
    far_last, x_own, d_own, _ = lax.optimization_barrier((far_last, x_own, d_own, (from_y, from_x, from_d)))
    last_far_core = to_lat(far_last, C_STEP)
    x_core = to_lat(x_own, C_STEP)
    d_core = to_lat(d_own, C_STEP)
    operands = (act, act_x, half, far, far_last, far_core, last_far_core, x_own, x_core, d_own, d_core)
    outs = [((2, 64, depth), bf16), ((1, 64, depth), bf16), ((1, 2, 64, depth), bf16)]
    grad_same, grad_next, grad_cross = pl.pallas_call(
        decoder_grad_kernel,
        name="decoder_grad",
        out_shape=[jax.ShapeDtypeStruct(shape, dtype) for shape, dtype in outs],
        in_specs=[VMEM] * len(operands),
        out_specs=[pl.BlockSpec(memory_space=pl.ANY)] * len(outs),
        scratch_shapes=[
            pltpu.VMEM((2, 128, depth), bf16),
            pltpu.VMEM((128, depth), bf16),
            pltpu.VMEM((5, 64, depth), bf16),
            pltpu.SemaphoreType.DMA((5,)),
        ],
        compiler_params=pltpu.CompilerParams(vmem_limit_bytes=48 * 1024 * 1024),
    )(*operands)
    return (mean_square[0, 0], jnp.swapaxes(grad_enc, 1, 2), grad_bias, grad_same, grad_next, grad_cross)


def shifted(value, axis, steps):
    count = lax.axis_size(axis)
    first, last = (max(0, -steps), min(count, count - steps))
    return lax.ppermute(value, axis, [(source, source + steps) for source in range(first, last)])


def back_dot(grad, weights):
    return lax.dot_general(
        grad, weights, (((1,), (1,)), ((), ())), preferred_element_type=jnp.float32
    )


def outer_dot(act, grad):
    return lax.dot_general(act, grad, (((0,), (0,)), ((), ())), preferred_element_type=jnp.float32)


def plain(resid_in, mlp_out, enc_weight, enc_bias, thresholds, same_dec, next_dec, cross_dec):
    leading = lax.axis_index("sec") == 0
    inputs_full = lax.all_gather(resid_in, "lat", axis=2, tiled=True)
    pre_act = (
        jnp.einsum("ktd,kdc->ktc", inputs_full, enc_weight, preferred_element_type=jnp.float32)
        + enc_bias[:, None, :]
    )
    cut_level = 0.25 * thresholds.astype(jnp.float32)[:, None, :]
    gate_value = jax.nn.sigmoid((pre_act - cut_level) / jump_width)
    latent_act = (pre_act * gate_value).astype(jnp.bfloat16)
    rebuilt_first = jnp.dot(latent_act[0], same_dec[0], preferred_element_type=jnp.float32)
    rebuilt_second = jnp.dot(
        latent_act[1], same_dec[1], preferred_element_type=jnp.float32
    ) + jnp.dot(latent_act[0], next_dec[0], preferred_element_type=jnp.float32)
    far_weight = shifted(cross_dec, "sec", -1)
    source_act = jnp.where(leading, latent_act, jnp.zeros_like(latent_act))
    near_part = jnp.einsum(
        "ktc,kcd->td", source_act, cross_dec[0], preferred_element_type=jnp.float32
    )
    far_part = jnp.einsum(
        "ktc,kcd->td", source_act, far_weight[0], preferred_element_type=jnp.float32
    )
    partials = jnp.stack([rebuilt_first, rebuilt_second, near_part, far_part])
    summed = lax.psum_scatter(partials, "lat", scatter_dimension=2, tiled=True)
    crossing = shifted(summed[2:], "sec", 1)
    rebuilt = summed[:2] + crossing
    misfit = rebuilt - mlp_out.astype(jnp.float32)
    squared_total = lax.psum(jnp.sum(misfit * misfit), ("sec", "lat"))
    mean_square = squared_total / (2.0 * mlp_out.size * lax.axis_size("lat"))
    dy_rows = misfit.astype(jnp.bfloat16)
    extra_rows = shifted(dy_rows, "sec", -1)
    grad_full = lax.all_gather(
        jnp.concatenate([dy_rows, extra_rows], axis=0), "lat", axis=2, tiled=True
    )
    act_grad = jnp.stack(
        [
            back_dot(grad_full[0], same_dec[0]) + back_dot(grad_full[1], next_dec[0]),
            back_dot(grad_full[1], same_dec[1]),
        ]
    )
    cross_grad = jnp.einsum(
        "td,kcd->ktc", grad_full[2], cross_dec[0], preferred_element_type=jnp.float32
    )
    cross_grad = cross_grad + jnp.einsum(
        "td,kcd->ktc", grad_full[3], far_weight[0], preferred_element_type=jnp.float32
    )
    act_grad = act_grad + cross_grad
    gate_slope = gate_value + pre_act * gate_value * (1.0 - gate_value) / jump_width
    pre_grad = act_grad * gate_slope
    grad_bias = jnp.sum(pre_grad, axis=1)
    pre_rounded = pre_grad.astype(jnp.bfloat16)
    grad_enc = jnp.einsum(
        "ktd,ktc->kdc", inputs_full, pre_rounded, preferred_element_type=jnp.float32
    ).astype(jnp.bfloat16)
    grad_same = jnp.stack(
        [outer_dot(latent_act[0], grad_full[0]), outer_dot(latent_act[1], grad_full[1])]
    ).astype(jnp.bfloat16)
    grad_next = outer_dot(latent_act[0], grad_full[1])[None].astype(jnp.bfloat16)
    near_grad = jnp.einsum(
        "ktc,td->kcd", source_act, grad_full[2], preferred_element_type=jnp.float32
    ).astype(jnp.bfloat16)
    far_grad = jnp.einsum(
        "ktc,td->kcd", source_act, grad_full[3], preferred_element_type=jnp.float32
    ).astype(jnp.bfloat16)
    far_back = shifted(far_grad, "sec", 1)
    grad_cross = jnp.where(leading, near_grad, far_back)[None]
    return (mean_square, grad_enc, grad_bias, grad_same, grad_next, grad_cross)


def solution(mesh):
    body = staged if mesh.shape["lat"] == 16 else plain
    in_specs = (
        P("sec", None, "lat"),
        P("sec", None, "lat"),
        P("sec", None, "lat"),
        P("sec", "lat"),
        P("sec", "lat"),
        P("sec", "lat", None),
        P("sec", "lat", None),
        P("sec", None, "lat", None),
    )
    out_specs = (
        P(),
        P("sec", None, "lat"),
        P("sec", "lat"),
        P("sec", "lat", None),
        P("sec", "lat", None),
        P("sec", None, "lat", None),
    )
    return jax.shard_map(body, mesh=mesh, in_specs=in_specs, out_specs=out_specs, check_vma=False)
```

```python
import functools

import jax
import jax.numpy as jnp
from jax import lax
from jax.experimental import pallas as pl
from jax.experimental.pallas import tpu as pltpu
from jax.sharding import PartitionSpec as P

jump_width = 0.1

Z_STEP, Y_STEP, C_STEP = 4, 2, 1

VMEM = pl.BlockSpec(memory_space=pltpu.VMEM)


def dot_nt(a, b):
    return lax.dot_general(a, b, (((1,), (1,)), ((), ())), preferred_element_type=jnp.float32)


def dot_tn(a, b):
    return lax.dot_general(a, b, (((0,), (0,)), ((), ())), preferred_element_type=jnp.float32)


def dot_nn(a, b):
    return lax.dot_general(a, b, (((1,), (0,)), ((), ())), preferred_element_type=jnp.float32)


def place():
    lat = lax.axis_index("lat")
    return lat // Z_STEP, (lat // Y_STEP) % 2, lat % 2


def lanes(start, size):
    return pl.ds(pl.multiple_of(start, 128), size)


def run(kernel, name, outs, *operands, cost=(0, 0)):
    return pl.pallas_call(
        kernel,
        name=name,
        out_shape=[jax.ShapeDtypeStruct(shape, dtype) for shape, dtype in outs],
        in_specs=[VMEM] * len(operands),
        out_specs=[VMEM] * len(outs),
        compiler_params=pltpu.CompilerParams(vmem_limit_bytes=48 * 1024 * 1024),
        cost_estimate=pl.CostEstimate(flops=cost[0], bytes_accessed=cost[1], transcendentals=0),
    )(*operands)


def to_lat(value, step):
    return lax.ppermute(value, "lat", [(source, source ^ step) for source in range(lax.axis_size("lat"))])


def to_both(value, sec_pairs, step):
    count = lax.axis_size("lat")
    pairs = [(a * count + lat, b * count + (lat ^ step)) for a, b in sec_pairs for lat in range(count)]
    return lax.ppermute(value, ("sec", "lat"), pairs)


SWAP = [(0, 1), (1, 0)]


def pack_kernel(same, nxt, cross, own_s, own_x, far_s, far_x, same_v, nxt_v, cross_v, sems):
    _, y, _ = place()
    width = own_s.shape[-1] // 4
    copies = [
        pltpu.make_async_copy(source, target, sems.at[n])
        for n, (source, target) in enumerate(((cross.at[0], cross_v), (same, same_v), (nxt.at[0], nxt_v)))
    ]
    for copy in copies:
        copy.start()

    def move(source, plain, row, crossed):
        for z in range(4):
            to = slice(z * width, (z + 1) * width)
            for half, out in enumerate((plain, crossed)):
                out[row, :, to] = source[:, lanes(z * 2 * width + (y + half) % 2 * width, width)]

    copies[0].wait()
    for j in range(2):
        move(cross_v.at[j], own_x, j, far_x)
    copies[1].wait()
    for layer in range(2):
        move(same_v.at[layer], own_s, layer, far_s)
    copies[2].wait()
    move(nxt_v, own_s, 2, far_s)


def stacked(ref, first, last):
    return ref[first:last].reshape((last - first) * ref.shape[1], ref.shape[2])


def pair_kernel(own, other, pair):
    pair[0] = own[...]
    pair[1] = other[...]


def relay_kernel(line1, line3, lines):
    lines[0] = line1[...]
    lines[1] = line3[...]


def row_kernel(one, two, row):
    row[0] = one[...]
    row[1] = two[...]


def last_kernel(own, line1, line2, line3, row, lead):
    row[0] = line2[...]
    row[1] = line3[...]
    for k, part in enumerate((own, line1, line2, line3)):
        lead[k] = part[0]


def encode_kernel(*refs):
    pieces, (weight, bias, cut, full, slope, act) = refs[:8], refs[8:]
    z, y, c = place()
    block = pieces[0].shape[-1]

    def put(k, j, core, layer, value):
        home = (z ^ k) * Z_STEP + (y ^ j) * Y_STEP + (c ^ core)
        full[layer, :, lanes(home * block, block)] = value

    for core in range(2):
        mine, lines, line2, line2_y = pieces[core * 4 : core * 4 + 4]
        for layer in range(2):
            for j in range(2):
                put(0, j, core, layer, mine[j, layer])
                put(1, j, core, layer, lines[0, j, layer])
                put(3, j, core, layer, lines[1, j, layer])
            put(2, 0, core, layer, line2[layer])
            put(2, 1, core, layer, line2_y[layer])
    for layer in range(2):
        pre = dot_nt(weight[layer], full[layer]) + bias[layer]
        gate = jax.nn.sigmoid((pre - cut[layer]) / jump_width)
        act[layer] = (pre * gate).astype(jnp.bfloat16)
        slope[layer] = gate + pre * gate * (1.0 - gate) / jump_width


def decode_kernel(act, act_y, act_x, act_d, own_s, own_x, peer_s, peer_x, near_x, diag_x, send, keep):
    _, _, c = place()
    leading = lax.axis_index("sec") == 0
    across, diagonal = (
        jnp.where(leading, jnp.zeros((128, 128), jnp.bfloat16), stacked(ref, 0, 2)) for ref in (act_x, act_d)
    )
    first = dot_tn(jnp.concatenate([act[0], act_y[0]]), jnp.concatenate([own_s[0], peer_s[0]]))
    first += dot_tn(across, stacked(near_x, 0, 2))
    first += dot_tn(diagonal, stacked(diag_x, 0, 2))
    second = dot_tn(jnp.concatenate([act[1], act[0]]), stacked(own_s, 1, 3))
    second += dot_tn(jnp.concatenate([act_y[1], act_y[0]]), stacked(peer_s, 1, 3))
    second += dot_tn(across, stacked(own_x, 0, 2))
    second += dot_tn(diagonal, stacked(peer_x, 0, 2))
    block = send.shape[-1]
    for layer, total in enumerate((first, second)):
        for z in range(4):
            low = total[:, z * 2 * block : z * 2 * block + block]
            high = total[:, z * 2 * block + block : (z + 1) * 2 * block]
            keep[z, layer] = jnp.where(c == 0, low, high)
            send[z, layer] = jnp.where(c == 0, high, low).astype(jnp.bfloat16)


def fold_kernel(keep, got, mine, s1, s2, s3):
    z, _, _ = place()
    mine[...] = keep[z] + got[z].astype(jnp.float32)
    for k, out in ((1, s1), (2, s2), (3, s3)):
        out[...] = (keep[z ^ k] + got[z ^ k].astype(jnp.float32)).astype(jnp.bfloat16)


def misfit_kernel(mine, g1, g2, g3, target, dy):
    total = mine[...] + g1[...].astype(jnp.float32) + g2[...].astype(jnp.float32) + g3[...].astype(jnp.float32)
    dy[...] = (total - target[...].astype(jnp.float32)).astype(jnp.bfloat16)


def act_grad_kernel(near, near_core, last, last_core, own_s, own_x, peer_s, peer_x, near_x, diag_x, half, grad_own, to_y, to_x, to_d):
    z, _, c = place()
    block = near.shape[-1]
    for k in range(4):
        mine, core = ((near, near_core), (last, last_core))[k // 2]
        for layer in range(2):
            half[layer, :, lanes(((z ^ k) * 2 + c) * block, block)] = mine[k % 2, layer]
            half[layer, :, lanes(((z ^ k) * 2 + 1 - c) * block, block)] = core[k % 2, layer]
    first, second = half[0], half[1]
    a = dot_nt(stacked(own_s, 1, 3), second)
    grad_own[0] = a[64:128] + dot_nt(own_s[0], first)
    grad_own[1] = a[0:64]
    a = dot_nt(stacked(peer_s, 1, 3), second)
    to_y[0:64] = (a[64:128] + dot_nt(peer_s[0], first)).astype(jnp.bfloat16)
    to_y[64:128] = a[0:64].astype(jnp.bfloat16)
    to_x[0:128] = (dot_nt(stacked(own_x, 0, 2), second) + dot_nt(stacked(near_x, 0, 2), first)).astype(jnp.bfloat16)
    to_d[0:128] = (dot_nt(stacked(peer_x, 0, 2), second) + dot_nt(stacked(diag_x, 0, 2), first)).astype(jnp.bfloat16)
    wide = half[...].astype(jnp.float32)
    squares = jnp.sum((wide * wide).reshape(-1, 8, wide.shape[-1]), axis=0)
    part = sum(squares[:, n * 128 : n * 128 + 128] for n in range(squares.shape[1] // 128))
    high = part.astype(jnp.bfloat16)
    low = (part - high.astype(jnp.float32)).astype(jnp.bfloat16)
    for out in (to_y, to_x, to_d):
        out[128:144] = jnp.concatenate([high, low])
    grad_own[2, 0:8] = part


def encoder_grad_kernel(entries, grad_own, from_y, from_x, from_d, slope, full, mean_square, grad_enc, grad_bias):
    leading = lax.axis_index("sec") == 0
    wide = [ref[...].astype(jnp.float32) for ref in (from_y, from_x, from_d)]
    squares = grad_own[2, 0:8] + sum(part[128:136] + part[136:144] for part in wide)
    mean_square[...] = jnp.sum(squares, keepdims=True) / entries
    for layer in range(2):
        rows = slice(layer * 64, layer * 64 + 64)
        across = wide[1][rows] + wide[2][rows]
        total = grad_own[layer] + wide[0][rows] + jnp.where(leading, across, jnp.zeros_like(across))
        pre_grad = total * slope[layer]
        grad_bias[layer : layer + 1] = jnp.sum(pre_grad.T, axis=0, keepdims=True)
        grad_enc[layer] = dot_nn(pre_grad.astype(jnp.bfloat16), full[layer]).astype(jnp.bfloat16)


def decoder_grad_kernel(act, act_x, half, far, last, far_core, last_core, x_own, x_core, d_own, d_core, grad_same, grad_next, grad_cross, dy, dx, staged_out, sems):
    z, y, c = place()
    leading = lax.axis_index("sec") == 0
    block = far.shape[-1]
    for layer in range(2):
        for n in range(4):
            dy[layer, :, lanes((n * 2 + y) * 2 * block, 2 * block)] = half[layer, :, n * 2 * block : (n + 1) * 2 * block]
        for k in range(4):
            home = (z ^ k) * Z_STEP + (1 - y) * Y_STEP
            mine, core = ((far, far_core), (last, last_core))[k // 2]
            dy[layer, :, lanes((home + c) * block, block)] = mine[k % 2, layer]
            dy[layer, :, lanes((home + 1 - c) * block, block)] = core[k % 2, layer]
    copies = []

    def out(value, stage, target):
        stage[...] = value.astype(jnp.bfloat16)
        copies.append(pltpu.make_async_copy(stage, target, sems.at[len(copies)]))
        copies[-1].start()

    both = jnp.concatenate([act[0], act[1]])
    second = dot_nn(both, dy[1])
    out(second[0:64], staged_out.at[0], grad_next.at[0])
    out(second[64:128], staged_out.at[1], grad_same.at[1])
    out(dot_nn(act[0], dy[0]), staged_out.at[2], grad_same.at[0])

    @pl.when(leading)
    def _():
        for k in range(4):
            for row, own, core in ((y, x_own, x_core), (1 - y, d_own, d_core)):
                home = (z ^ k) * Z_STEP + row * Y_STEP
                dx[:, lanes((home + c) * block, block)] = own[k]
                dx[:, lanes((home + 1 - c) * block, block)] = core[k]

    @pl.when(jnp.logical_not(leading))
    def _():
        dx[...] = dy[1]

    source = jnp.where(leading, both, stacked(act_x, 0, 2))
    for j in range(2):
        out(dot_nn(source[j * 64 : j * 64 + 64], dx[...]), staged_out.at[3 + j], grad_cross.at[0, j])
    for copy in copies:
        copy.wait()


def staged(resid_in, mlp_out, enc_weight, enc_bias, thresholds, same_dec, next_dec, cross_dec):
    bf16, f32 = jnp.bfloat16, jnp.float32
    depth = same_dec.shape[-1]
    block = resid_in.shape[-1]
    entries = 2.0 * resid_in.size * lax.axis_size("lat")
    tall = jnp.swapaxes(enc_weight, 1, 2)
    bias = jnp.broadcast_to(enc_bias[:, :, None], (2, 64, 128))
    cut = jnp.broadcast_to(0.25 * thresholds.astype(f32)[:, :, None], (2, 64, 128))

    other = to_lat(resid_in, Y_STEP)
    line2 = to_lat(resid_in, 2 * Z_STEP)
    shapes = [((3, 64, depth // 2), bf16), ((2, 64, depth // 2), bf16)] * 2
    own_s, own_x, far_s, far_x = pl.pallas_call(
        pack_kernel,
        name="pack",
        out_shape=[jax.ShapeDtypeStruct(shape, dtype) for shape, dtype in shapes],
        in_specs=[pl.BlockSpec(memory_space=pl.ANY)] * 3,
        out_specs=[VMEM] * 4,
        scratch_shapes=[
            pltpu.VMEM((2, 64, depth), bf16),
            pltpu.VMEM((64, depth), bf16),
            pltpu.VMEM((2, 64, depth), bf16),
            pltpu.SemaphoreType.DMA((3,)),
        ],
    )(same_dec, next_dec, cross_dec)
    (near,) = run(pair_kernel, "pair", [((2, 2, 128, block), bf16)], resid_in, other)
    line1, line3 = (to_lat(near, k * Z_STEP) for k in (1, 3))
    line2, far_x, _ = lax.optimization_barrier((line2, far_x, near))
    line2_y = to_lat(line2, Y_STEP)
    peer_x = to_lat(far_x, Y_STEP)
    lead_x, _ = lax.optimization_barrier((own_x, other))
    near_x = to_both(lead_x, SWAP, 0)
    far_s, line2_y = lax.optimization_barrier((far_s, line2_y))
    peer_s = to_lat(far_s, Y_STEP)
    diag_x = to_both(peer_x, SWAP, 0)
    (lines,) = run(relay_kernel, "relay", [((2, 2, 2, 128, block), bf16)], line1, line3, cost=(1_000_000_000, 0))
    lines, near_x, bias, cut = lax.optimization_barrier((lines, near_x, bias, cut))
    pieces = [near, lines, line2, line2_y]
    pieces += [to_lat(piece, C_STEP) for piece in pieces]
    full, slope, act = run(
        encode_kernel, "encode",
        [((2, 128, depth), bf16), ((2, 64, 128), f32), ((2, 64, 128), bf16)],
        *pieces, tall, bias, cut,
    )
    act_y = to_lat(act, Y_STEP)
    act_x = to_both(act, SWAP, 0)
    act_d = to_both(act, SWAP, Y_STEP)
    send, keep = run(
        decode_kernel, "decode",
        [((4, 2, 128, block), bf16), ((4, 2, 128, block), f32)],
        act, act_y, act_x, act_d, own_s, own_x, peer_s, peer_x, near_x, diag_x,
    )
    got = to_lat(send, C_STEP)
    mine, *parts = run(
        fold_kernel, "fold",
        [((2, 128, block), f32)] + [((2, 128, block), bf16)] * 3,
        keep, got,
    )
    parts = [to_lat(part, k * Z_STEP) for k, part in zip((1, 2, 3), parts)]
    (dy,) = run(misfit_kernel, "misfit", [((2, 128, block), bf16)], mine, *parts, mlp_out)
    pair = ((2, 2, 128, block), bf16)
    line1, line2, line3 = (to_lat(dy, k * Z_STEP) for k in (1, 2, 3))
    (row,) = run(row_kernel, "row", [pair], dy, line1)
    far = to_lat(row, Y_STEP)
    row_core = to_lat(row, C_STEP)
    last, lead = run(last_kernel, "last", [pair, ((4, 128, block), bf16)], dy, line1, line2, line3, cost=(2_000_000_000, 0))
    last, lead, far = lax.optimization_barrier((last, lead, far))
    far_core = to_lat(far, C_STEP)
    last_core = to_lat(last, C_STEP)
    far_last = to_lat(last, Y_STEP)
    x_own = to_both(lead, SWAP, 0)
    d_own = to_both(lead, SWAP, Y_STEP)
    half, grad_own, to_y, to_x, to_d = run(
        act_grad_kernel, "act_grad",
        [((2, 128, depth // 2), bf16), ((3, 64, 128), f32)] + [((144, 128), bf16)] * 3,
        row, row_core, last, last_core, own_s, own_x, peer_s, peer_x, near_x, diag_x,
    )
    from_y = to_lat(to_y, Y_STEP)
    from_x = to_both(to_x, SWAP, 0)
    from_d = to_both(to_d, SWAP, Y_STEP)
    mean_square, grad_enc, grad_bias = run(
        functools.partial(encoder_grad_kernel, entries), "encoder_grad",
        [((1, 1), f32), ((2, 64, depth), bf16), ((2, 64), f32)],
        grad_own, from_y, from_x, from_d, slope, full,
    )
    far_last, x_own, d_own, _ = lax.optimization_barrier((far_last, x_own, d_own, (from_y, from_x, from_d)))
    last_far_core = to_lat(far_last, C_STEP)
    x_core = to_lat(x_own, C_STEP)
    d_core = to_lat(d_own, C_STEP)
    operands = (act, act_x, half, far, far_last, far_core, last_far_core, x_own, x_core, d_own, d_core)
    outs = [((2, 64, depth), bf16), ((1, 64, depth), bf16), ((1, 2, 64, depth), bf16)]
    grad_same, grad_next, grad_cross = pl.pallas_call(
        decoder_grad_kernel,
        name="decoder_grad",
        out_shape=[jax.ShapeDtypeStruct(shape, dtype) for shape, dtype in outs],
        in_specs=[VMEM] * len(operands),
        out_specs=[pl.BlockSpec(memory_space=pl.ANY)] * len(outs),
        scratch_shapes=[
            pltpu.VMEM((2, 128, depth), bf16),
            pltpu.VMEM((128, depth), bf16),
            pltpu.VMEM((5, 64, depth), bf16),
            pltpu.SemaphoreType.DMA((5,)),
        ],
        compiler_params=pltpu.CompilerParams(vmem_limit_bytes=48 * 1024 * 1024),
    )(*operands)
    return (mean_square[0, 0], jnp.swapaxes(grad_enc, 1, 2), grad_bias, grad_same, grad_next, grad_cross)


def shifted(value, axis, steps):
    count = lax.axis_size(axis)
    first, last = (max(0, -steps), min(count, count - steps))
    return lax.ppermute(value, axis, [(source, source + steps) for source in range(first, last)])


def back_dot(grad, weights):
    return lax.dot_general(
        grad, weights, (((1,), (1,)), ((), ())), preferred_element_type=jnp.float32
    )


def outer_dot(act, grad):
    return lax.dot_general(act, grad, (((0,), (0,)), ((), ())), preferred_element_type=jnp.float32)


def plain(resid_in, mlp_out, enc_weight, enc_bias, thresholds, same_dec, next_dec, cross_dec):
    leading = lax.axis_index("sec") == 0
    inputs_full = lax.all_gather(resid_in, "lat", axis=2, tiled=True)
    pre_act = (
        jnp.einsum("ktd,kdc->ktc", inputs_full, enc_weight, preferred_element_type=jnp.float32)
        + enc_bias[:, None, :]
    )
    cut_level = 0.25 * thresholds.astype(jnp.float32)[:, None, :]
    gate_value = jax.nn.sigmoid((pre_act - cut_level) / jump_width)
    latent_act = (pre_act * gate_value).astype(jnp.bfloat16)
    rebuilt_first = jnp.dot(latent_act[0], same_dec[0], preferred_element_type=jnp.float32)
    rebuilt_second = jnp.dot(
        latent_act[1], same_dec[1], preferred_element_type=jnp.float32
    ) + jnp.dot(latent_act[0], next_dec[0], preferred_element_type=jnp.float32)
    far_weight = shifted(cross_dec, "sec", -1)
    source_act = jnp.where(leading, latent_act, jnp.zeros_like(latent_act))
    near_part = jnp.einsum(
        "ktc,kcd->td", source_act, cross_dec[0], preferred_element_type=jnp.float32
    )
    far_part = jnp.einsum(
        "ktc,kcd->td", source_act, far_weight[0], preferred_element_type=jnp.float32
    )
    partials = jnp.stack([rebuilt_first, rebuilt_second, near_part, far_part])
    summed = lax.psum_scatter(partials, "lat", scatter_dimension=2, tiled=True)
    crossing = shifted(summed[2:], "sec", 1)
    rebuilt = summed[:2] + crossing
    misfit = rebuilt - mlp_out.astype(jnp.float32)
    squared_total = lax.psum(jnp.sum(misfit * misfit), ("sec", "lat"))
    mean_square = squared_total / (2.0 * mlp_out.size * lax.axis_size("lat"))
    dy_rows = misfit.astype(jnp.bfloat16)
    extra_rows = shifted(dy_rows, "sec", -1)
    grad_full = lax.all_gather(
        jnp.concatenate([dy_rows, extra_rows], axis=0), "lat", axis=2, tiled=True
    )
    act_grad = jnp.stack(
        [
            back_dot(grad_full[0], same_dec[0]) + back_dot(grad_full[1], next_dec[0]),
            back_dot(grad_full[1], same_dec[1]),
        ]
    )
    cross_grad = jnp.einsum(
        "td,kcd->ktc", grad_full[2], cross_dec[0], preferred_element_type=jnp.float32
    )
    cross_grad = cross_grad + jnp.einsum(
        "td,kcd->ktc", grad_full[3], far_weight[0], preferred_element_type=jnp.float32
    )
    act_grad = act_grad + cross_grad
    gate_slope = gate_value + pre_act * gate_value * (1.0 - gate_value) / jump_width
    pre_grad = act_grad * gate_slope
    grad_bias = jnp.sum(pre_grad, axis=1)
    pre_rounded = pre_grad.astype(jnp.bfloat16)
    grad_enc = jnp.einsum(
        "ktd,ktc->kdc", inputs_full, pre_rounded, preferred_element_type=jnp.float32
    ).astype(jnp.bfloat16)
    grad_same = jnp.stack(
        [outer_dot(latent_act[0], grad_full[0]), outer_dot(latent_act[1], grad_full[1])]
    ).astype(jnp.bfloat16)
    grad_next = outer_dot(latent_act[0], grad_full[1])[None].astype(jnp.bfloat16)
    near_grad = jnp.einsum(
        "ktc,td->kcd", source_act, grad_full[2], preferred_element_type=jnp.float32
    ).astype(jnp.bfloat16)
    far_grad = jnp.einsum(
        "ktc,td->kcd", source_act, grad_full[3], preferred_element_type=jnp.float32
    ).astype(jnp.bfloat16)
    far_back = shifted(far_grad, "sec", 1)
    grad_cross = jnp.where(leading, near_grad, far_back)[None]
    return (mean_square, grad_enc, grad_bias, grad_same, grad_next, grad_cross)


def solution(mesh):
    body = staged if mesh.shape["lat"] == 16 else plain
    in_specs = (
        P("sec", None, "lat"),
        P("sec", None, "lat"),
        P("sec", None, "lat"),
        P("sec", "lat"),
        P("sec", "lat"),
        P("sec", "lat", None),
        P("sec", "lat", None),
        P("sec", None, "lat", None),
    )
    out_specs = (
        P(),
        P("sec", None, "lat"),
        P("sec", "lat"),
        P("sec", "lat", None),
        P("sec", "lat", None),
        P("sec", None, "lat", None),
    )
    return jax.shard_map(body, mesh=mesh, in_specs=in_specs, out_specs=out_specs, check_vma=False)
```
